256 devices in a mesh: tok: 128 (over x_hi, y, z, core), head: 2 (over x_lo).
Axes of the slice: x: 4 (x_hi: 2, x_lo: 2; x = x_hi * 2 + x_lo), y: 4, z: 8, core: 2. Of those that a mesh axis runs over, the one named last changes fastest.
Arguments:
- tokens: bfloat16 [16384, 768], P('tok', 'head'), may hold values from -64 to 64
- view_ids: int32 [16384], P('tok'), may hold values from 0 to 19, never falling along the last dimension, each value on 1 to 1024 neighbouring positions
- query_weight: bfloat16 [768, 768], P(None, 'head'), may hold values from -0.21875 to 0.21875
- key_weight: bfloat16 [768, 768], P(None, 'head'), may hold values from -0.4375 to 0.4375
- value_weight: bfloat16 [768, 768], P(None, 'head'), may hold values from -0.21875 to 0.21875
- out_weight: bfloat16 [768, 768], P('head'), may hold values from -0.21875 to 0.21875
- rate_weight: bfloat16 [768, 4], P(None, 'head'), may hold values from -0.21875 to 0.21875
- fast_gate: float32 [4, 192, 384], P('head'), may hold values from -0.4375 to 0.4375
- fast_up: float32 [4, 192, 384], P('head'), may hold values from -0.4375 to 0.4375
- fast_down: float32 [4, 192, 384], P('head'), may hold values from -0.3125 to 0.3125
- step_size: float32 [4], P('head'), may hold values from 1 to 3
Outputs:
- layer_out: bfloat16 [16384, 768], P('tok', 'head')
The draws below stay inside these ranges and needn't reach their ends.
Inputs may be any that keep to these rules, and one draw needn't show every extreme that they name: `view_ids`: Non-decreasing along the tokens; every view number appears, on one contiguous run of 1 to 1024 tokens, and some view has exactly 1024.
All inputs are finite; a program needn't handle non-finite values.
Results may differ from the reference program's by a relative error of at most 0.014.
The reference program's roundings to bfloat16 on the way (of `lowered`, `product`, `error`, `fresh` and `mixed`) count: a program that leaves them out, or rounds other values in their place, can miss the bound.
Values may be sent and summed in bfloat16 or wider, within the bound.
No kernel may reach another device: no remote copies, remote signals or barrier semaphores. Data moves between devices by JAX's collectives and lax.ppermute only.
A program may use at most 64 MiB of HBM per device.

```python
import math
import jax
import jax.numpy as jnp
import numpy as np
from jax import lax

D = 768
HEADS = 4
FH = 384
NS_STEPS = 5
TOK_DEV = 128
DH = 192
TOKENS = 16384
VIEW_SPAN = 8
VIEWS = 20
N_TOK = 128


def draw_tokens(key, part):
    first_key = jax.random.fold_in(jax.random.fold_in(key, 11), 0)
    base = jnp.clip(jax.random.normal(first_key, (TOKENS, D), jnp.float32), -6.0, 6.0)
    return base.astype(jnp.bfloat16)


def steps_of(own_key, dims, shards, smallest, high):
    gain = 1.0
    for position, parts in shards:
        heights = jax.random.uniform(jax.random.fold_in(jax.random.fold_in(own_key, 6), position), (parts,), jnp.float32, smallest / len(shards), high / len(shards))
        gain = gain * jnp.repeat(jnp.exp(heights), dims[position] // parts).reshape((-1,) + (1,) * (len(dims) - 1 - position))
    return gain


def split_up(amount, total, most, lean):
    portions = [(1 << 20) // math.isqrt(rank ** lean) + 1 for rank in range(2, amount + 1)]
    rest, given = total - most - (amount - 1), [1] * (amount - 1)
    while rest > 0:
        movable = [i for i in range(amount - 1) if given[i] < most]
        pool, remaining = sum([portions[i] for i in movable]), rest
        for i in movable:
            addition = min(most - given[i], max(1, remaining * portions[i] // pool), rest)
            given[i] = given[i] + addition
            rest = rest - addition
    return np.array([most] + given)


def uneven_parts(stream_key, amount, total, bound, slope):
    if amount == 2:
        one = jax.random.randint(stream_key, (), max(1, total - bound), min(bound, total - 1) + 1)
        return jnp.stack([one, total - one])
    tallies = jnp.asarray(split_up(amount, total, bound, slope), jnp.int32)
    couples = (amount - 1) // 2
    giver, receiver = tallies[1:1 + 2 * couples:2], tallies[2:2 + 2 * couples:2]
    slack = jnp.minimum(giver - 1, bound - receiver)
    moved = jax.random.randint(jax.random.fold_in(stream_key, 1), (couples,), 0, 1 << 20) % (slack + 1)
    tallies = tallies.at[1:1 + 2 * couples:2].set(giver - moved).at[2:2 + 2 * couples:2].set(receiver + moved)
    return tallies[jax.random.permutation(jax.random.fold_in(stream_key, 2), amount)]


def bell_draw(own_key, dims, scale, reach, pieces=(), held_as=jnp.bfloat16):
    loudness = steps_of(own_key, dims, pieces, -0.22, 0.18) if pieces else 1.0
    drawn = jax.random.normal(own_key, dims, jnp.float32) * scale * loudness
    return jnp.minimum(jnp.maximum(drawn, -reach), reach).astype(held_as)


def setup_inputs(seed: int = 0) -> dict:
    streams_of = jax.random.split(jax.random.key(seed), 12)
    tokens = draw_tokens(jax.random.fold_in(streams_of[11], 71), 0)
    view_ids = jnp.searchsorted(jnp.cumsum(uneven_parts(streams_of[1], VIEWS, TOKENS, VIEW_SPAN * TOK_DEV, 0)), jnp.arange(TOKENS), side="right").astype(jnp.int32)
    query_weight = bell_draw(streams_of[2], (D, D), D ** -0.5, 0.21875, ((1, 2),))
    key_weight = bell_draw(streams_of[3], (D, D), (D // 4) ** -0.5, 0.4375, ((1, 2),))
    value_weight = bell_draw(streams_of[4], (D, D), D ** -0.5, 0.21875, ((1, 2),))
    out_weight = bell_draw(streams_of[5], (D, D), D ** -0.5, 0.21875, ((0, 2),))
    rate_weight = bell_draw(streams_of[6], (D, HEADS), D ** -0.5, 0.21875, ((1, 2),))
    fast_gate = bell_draw(streams_of[7], (HEADS, DH, FH), DH ** -0.5, 0.4375, ((0, 2),), jnp.float32)
    fast_up = bell_draw(streams_of[8], (HEADS, DH, FH), DH ** -0.5, 0.4375, ((0, 2),), jnp.float32)
    fast_down = bell_draw(streams_of[9], (HEADS, DH, FH), FH ** -0.5, 0.3125, ((0, 2),), jnp.float32)
    step_size = jnp.clip(jnp.exp(math.log(3.0) - 1.0986123 * jax.random.uniform(streams_of[10], (HEADS,), jnp.float32) ** steps_of(streams_of[10], (HEADS,), ((0, 2),), -0.2, 0.2)), 1.0, 3.0)
    return dict(tokens=tokens, view_ids=view_ids, query_weight=query_weight, key_weight=key_weight, value_weight=value_weight, out_weight=out_weight, rate_weight=rate_weight, fast_gate=fast_gate, fast_up=fast_up, fast_down=fast_down, step_size=step_size)


newton_a = 3.4445
newton_b = -4.775
newton_c = 2.0315
epsilon = 1e-06
masked_score = -1e+30

def normalize(values):
    widened = values.astype(jnp.float32)
    scale = lax.rsqrt(lax.optimization_barrier(jnp.mean(widened * widened, axis=-1, keepdims=True)) + epsilon)
    return (widened * scale).astype(jnp.bfloat16)

def orthogonalize(matrix):
    length = jnp.sqrt(lax.optimization_barrier(jnp.sum(matrix * matrix, axis=(-2, -1), keepdims=True)))
    current = matrix / (length + epsilon)
    for ns_step in range(NS_STEPS):
        square = jnp.einsum('...ik,...jk->...ij', current, current, precision=lax.Precision.HIGHEST)
        mixer = newton_b * square + newton_c * jnp.einsum('...ik,...kj->...ij', square, square, precision=lax.Precision.HIGHEST)
        current = newton_a * current + jnp.einsum('...ik,...kj->...ij', mixer, current, precision=lax.Precision.HIGHEST)
    return current

def fast_terms(keys_n, values, rates, lowered):
    widened = keys_n.astype(jnp.float32)
    gate = jnp.einsum('thd,hdf->thf', widened, lowered[:, 0].astype(jnp.float32))
    upward = jnp.einsum('thd,hdf->thf', widened, lowered[:, 1].astype(jnp.float32))
    active = jax.nn.silu(gate)
    product = (active * upward).astype(jnp.bfloat16)
    error = (-rates[:, :, None] * values.astype(jnp.float32)).astype(jnp.bfloat16)
    grad_down = jnp.einsum('thf,thd->hdf', product.astype(jnp.float32), error.astype(jnp.float32))
    back = jnp.einsum('thd,hdf->thf', error.astype(jnp.float32), lowered[:, 2].astype(jnp.float32))
    logistic = jax.nn.sigmoid(gate)
    grad_gate_in = (back * upward * logistic * (1.0 + gate * (1.0 - logistic))).astype(jnp.bfloat16)
    grad_up_in = (back * active).astype(jnp.bfloat16)
    grad_gate = jnp.einsum('thd,thf->hdf', widened, grad_gate_in.astype(jnp.float32))
    grad_up = jnp.einsum('thd,thf->hdf', widened, grad_up_in.astype(jnp.float32))
    return jnp.stack((grad_gate, grad_up, grad_down), 1)

def apply_fast(queries_n, fresh):
    widened = queries_n.astype(jnp.float32)
    gate = jnp.einsum('thd,hdf->thf', widened, fresh[:, 0].astype(jnp.float32))
    upward = jnp.einsum('thd,hdf->thf', widened, fresh[:, 1].astype(jnp.float32))
    product = (jax.nn.silu(gate) * upward).astype(jnp.bfloat16)
    return jnp.einsum('thf,hdf->thd', product.astype(jnp.float32), fresh[:, 2].astype(jnp.float32))

def attend(query_rows, key_rows, value_rows, query_view, key_view):
    scores = jnp.einsum('qhd,khd->hqk', query_rows.astype(jnp.float32), key_rows.astype(jnp.float32))
    scores = scores * query_rows.shape[2] ** (-0.5)
    allowed = (query_view[:, None] == key_view[None, :])[None]
    scores = jnp.where(allowed, scores, masked_score)
    peak = lax.optimization_barrier(jnp.max(scores, axis=-1, keepdims=True))
    weights = jnp.exp(scores - peak)
    weights = (weights / lax.optimization_barrier(jnp.sum(weights, axis=-1, keepdims=True))).astype(jnp.bfloat16)
    return jnp.einsum('hqk,khd->qhd', weights.astype(jnp.float32), value_rows.astype(jnp.float32))

def reference(tokens, view_ids, query_weight, key_weight, value_weight, out_weight, rate_weight, fast_gate, fast_up, fast_down, step_size):
    head_width = D // HEADS
    queries = jnp.dot(tokens, query_weight, preferred_element_type=jnp.float32).astype(jnp.bfloat16).reshape(TOKENS, HEADS, head_width)
    keys = jnp.dot(tokens, key_weight, preferred_element_type=jnp.float32).astype(jnp.bfloat16).reshape(TOKENS, HEADS, head_width)
    values = jnp.dot(tokens, value_weight, preferred_element_type=jnp.float32).astype(jnp.bfloat16).reshape(TOKENS, HEADS, head_width)
    rates = jax.nn.softplus(jnp.dot(tokens, rate_weight, preferred_element_type=jnp.float32))
    positions = jnp.arange(TOKENS, dtype=jnp.int32)
    rates = rates * (positions < 3 * TOKENS // 4).astype(jnp.float32)[:, None]
    keys_n = normalize(keys)
    queries_n = normalize(queries)
    master = jnp.stack((fast_gate, fast_up, fast_down), 1)
    lowered = master.astype(jnp.bfloat16)

    def slice_block(array, start):
        return lax.dynamic_slice_in_dim(array, start, TOK_DEV, 0)

    def accumulate(carry, block_index):
        start = block_index * TOK_DEV
        term = fast_terms(slice_block(keys_n, start), slice_block(values, start), slice_block(rates, start), lowered)
        return (carry + term, None)
    total, unused = lax.scan(accumulate, jnp.zeros(master.shape, jnp.float32), jnp.arange(N_TOK, dtype=jnp.int32))
    fresh = (master - step_size[:, None, None, None] * orthogonalize(total)).astype(jnp.bfloat16)
    margin_rows = VIEW_SPAN * TOK_DEV
    window_rows = (2 * VIEW_SPAN + 1) * TOK_DEV
    blank = jnp.zeros((margin_rows, HEADS, head_width), jnp.bfloat16)
    padded_keys = jnp.concatenate((blank, keys, blank), 0)
    padded_values = jnp.concatenate((blank, values, blank), 0)
    blank_views = jnp.full((margin_rows,), -1, jnp.int32)
    padded_views = jnp.concatenate((blank_views, view_ids.astype(jnp.int32), blank_views), 0)

    def output_block(block_index):
        start = block_index * TOK_DEV
        near_keys = lax.dynamic_slice_in_dim(padded_keys, start, window_rows, 0)
        near_values = lax.dynamic_slice_in_dim(padded_values, start, window_rows, 0)
        near_views = lax.dynamic_slice_in_dim(padded_views, start, window_rows, 0)
        attended = attend(slice_block(queries, start), near_keys, near_values, slice_block(view_ids, start), near_views)
        applied = apply_fast(slice_block(queries_n, start), fresh)
        mixed = (attended + applied).astype(jnp.bfloat16).reshape(TOK_DEV, D)
        return jnp.dot(mixed, out_weight, preferred_element_type=jnp.float32).astype(jnp.bfloat16)
    return lax.map(output_block, jnp.arange(N_TOK, dtype=jnp.int32)).reshape(TOKENS, D)
```

```python
import jax
import jax.numpy as jnp
from jax import lax
from jax.experimental import pallas as pl
from jax.experimental.pallas import tpu as pltpu
from jax.sharding import Mesh, PartitionSpec as P

NS_STEPS = 5
newton_a = 3.4445
newton_b = -4.775
newton_c = 2.0315
epsilon = 1e-06
masked_score = -1e30

TOK = ("xh", "y", "z", "core")
CHIPS = ("xh", "y", "z")
REACH = 4
DH = 192
FH = 384
f32 = jnp.float32
bf16 = jnp.bfloat16


def normalize(values):
    widened = values.astype(f32)
    scale = lax.rsqrt(jnp.mean(widened * widened, axis=-1, keepdims=True) + epsilon)
    return (widened * scale).astype(bf16)


def halves(x):
    high = x.astype(bf16)
    return high, (x - high.astype(f32)).astype(bf16)


def nt(a, b):
    return lax.dot_general(a, b, (((1,), (1,)), ((), ())), preferred_element_type=f32)


def nn(a, b):
    return lax.dot_general(a, b, (((1,), (0,)), ((), ())), preferred_element_type=f32)


def tn(a, b):
    return lax.dot_general(a, b, (((0,), (0,)), ((), ())), preferred_element_type=f32)


def fresh_kernel(total_ref, master_ref, step_ref, fresh_ref):
    step = step_ref[0, 0]
    currents = []
    for m in range(3):
        matrix = total_ref[m]
        length = jnp.sqrt(jnp.sum(matrix * matrix))
        currents.append(matrix / (length + epsilon))
    for _ in range(NS_STEPS):
        squares = []
        for x in currents:
            h, l = halves(x)
            squares.append((h, l, nt(h, h) + (nt(h, l) + nt(l, h))))
        mixers = []
        for h, l, a in squares:
            ah, al = halves(a)
            aa = nn(ah, ah) + (nn(ah, al) + nn(al, ah))
            mixers.append((h, l, newton_b * a + newton_c * aa))
        nexts = []
        for x, (h, l, b) in zip(currents, mixers):
            bh, bl = halves(b)
            nexts.append(newton_a * x + (nn(bh, h) + (nn(bh, l) + nn(bl, h))))
        currents = nexts
    for m in range(3):
        fresh_ref[m] = (master_ref[m] - step * currents[m]).astype(bf16)


def make_fresh(total, master, step):
    return pl.pallas_call(
        fresh_kernel,
        out_shape=jax.ShapeDtypeStruct((3, DH, FH), bf16),
        in_specs=[
            pl.BlockSpec(memory_space=pltpu.VMEM),
            pl.BlockSpec(memory_space=pltpu.VMEM),
            pl.BlockSpec(memory_space=pltpu.SMEM),
        ],
        out_specs=pl.BlockSpec(memory_space=pltpu.VMEM),
        name="fresh",
    )(total, master, step)


def hop(x, steps):
    return lax.ppermute(
        x, CHIPS, [(i, i + steps) for i in range(64) if 0 <= i + steps < 64]
    )


def body(
    tokens,
    view_ids,
    query_weight,
    key_weight,
    value_weight,
    out_weight,
    rate_weight,
    fast_gate,
    fast_up,
    fast_down,
    step_size,
):
    core = lax.axis_index("core")
    xl = lax.axis_index("xl")
    chip = (lax.axis_index("xh") * 4 + lax.axis_index("y")) * 8 + lax.axis_index("z")
    whole = lax.all_gather(tokens, ("xl", "core"), axis=0, tiled=True)
    features = jnp.concatenate((whole[:256], whole[256:]), 1)
    views = lax.all_gather(view_ids, "core", axis=0, tiled=True)

    def own_columns(w):
        return jnp.where(core == 0, w[:, :DH], w[:, DH:])

    def own(w):
        return lax.dynamic_index_in_dim(w, core, 0, keepdims=False)

    query = nn(features, own_columns(query_weight)).astype(bf16)
    key = nn(features, own_columns(key_weight)).astype(bf16)
    value = nn(features, own_columns(value_weight)).astype(bf16)
    rates = jax.nn.softplus(nn(features, rate_weight))
    rates = jnp.where(core == 0, rates[:, :1], rates[:, 1:])
    rates = rates * (chip < 48).astype(f32)

    tag = (views + 1).astype(bf16)
    tag_rows = jnp.zeros((16, 2 * DH), bf16).at[0, :256].set(tag)
    packed = jnp.concatenate((jnp.concatenate((key, value), 1), tag_rows), 0)
    pieces = [packed]
    ahead = behind = packed
    for _ in range(REACH):
        ahead, behind = hop(ahead, 1), hop(behind, -1)
        pieces += [ahead, behind]

    master = jnp.stack((own(fast_gate), own(fast_up), own(fast_down)), 0)
    lowered = master.astype(bf16)
    keys_n = normalize(key)
    gate = nn(keys_n, lowered[0])
    upward = nn(keys_n, lowered[1])
    logistic = jax.nn.sigmoid(gate)
    active = gate * logistic
    product = (active * upward).astype(bf16)
    error = (-rates * value.astype(f32)).astype(bf16)
    back = nn(error, lowered[2])
    grad_g = (back * upward * logistic * (1.0 + gate * (1.0 - logistic))).astype(bf16)
    grad_u = (back * active).astype(bf16)
    terms = jnp.concatenate((tn(keys_n, grad_g), tn(keys_n, grad_u), tn(error, product)), 0)

    sent = terms.reshape(8, 72, FH).astype(bf16)
    got = lax.all_to_all(sent, ("xh", "y"), 0, 0, tiled=True)
    part = jnp.sum(got.astype(f32), 0).astype(bf16)
    got = lax.all_to_all(jnp.broadcast_to(part[None], (8, 72, FH)), "z", 0, 0, tiled=True)
    part = jnp.sum(got.astype(f32), 0).astype(bf16)
    got = lax.all_to_all(
        jnp.broadcast_to(part[None], (8, 72, FH)), ("xh", "y"), 0, 0, tiled=True
    )
    total = got.astype(f32).reshape(3, DH, FH)
    fresh = make_fresh(total, master, own(step_size).reshape(1, 1))

    near = jnp.concatenate([p[:256] for p in pieces], 0)
    near_views = jnp.concatenate([p[256, :256] for p in pieces], 0)
    scores = nt(query, near[:, :DH]) * DH**-0.5
    scores = jnp.where(tag[:, None] == near_views[None, :], scores, masked_score)
    weights = jnp.exp(scores - jnp.max(scores, axis=-1, keepdims=True))
    weights = (weights / jnp.sum(weights, axis=-1, keepdims=True)).astype(bf16)
    attended = nn(weights, near[:, DH:])

    queries_n = normalize(query)
    gate = nn(queries_n, fresh[0])
    upward = nn(queries_n, fresh[1])
    applied = nt((jax.nn.silu(gate) * upward).astype(bf16), fresh[2])
    mixed = (attended + applied).astype(bf16)

    mine = lax.dynamic_slice_in_dim(out_weight, xl * FH, FH, 1)
    theirs = lax.dynamic_slice_in_dim(out_weight, (1 - xl) * FH, FH, 1)
    other = lax.ppermute(theirs, "xl", [(0, 1), (1, 0)])
    upper = jnp.where(xl == 0, mine, other)
    lower = jnp.where(xl == 0, other, mine)
    out_columns = jnp.concatenate((upper, lower), 0)

    spread = lax.all_gather(mixed, ("xl", "core"), axis=0)
    spread = lax.dynamic_slice_in_dim(spread, core * 128, 128, 1)
    side = jnp.concatenate([spread[h] for h in range(4)], 1)
    return nn(side, out_columns).astype(bf16)


def solution(mesh):
    fine = Mesh(mesh.devices.reshape(2, 4, 8, 2, 2), ("xh", "y", "z", "core", "xl"))
    placed = (
        P(TOK, "xl"),
        P(TOK),
        P(None, "xl"),
        P(None, "xl"),
        P(None, "xl"),
        P("xl", None),
        P(None, "xl"),
        P("xl", None, None),
        P("xl", None, None),
        P("xl", None, None),
        P("xl"),
    )
    return jax.shard_map(
        body, mesh=fine, in_specs=placed, out_specs=P(TOK, "xl"), check_vma=False
    )
```

```python
import jax
import jax.numpy as jnp
from jax import lax
from jax.experimental import pallas as pl
from jax.experimental.pallas import tpu as pltpu
from jax.sharding import Mesh, PartitionSpec as P


NS_STEPS = 5
newton_a = 3.4445
newton_b = -4.775
newton_c = 2.0315
epsilon = 1e-06
masked_score = -1e30

TOK = ("xh", "y", "z", "core")
CHIPS = ("xh", "y", "z")
REACH = 4
DH = 192
FH = 384
TOK_DEV = 128
ROWS = 2 * TOK_DEV
PACKED = ROWS + 16
GATHERED = TOK_DEV + 16
TAGS = 32
f32 = jnp.float32
bf16 = jnp.bfloat16
VMEM = pl.BlockSpec(memory_space=pltpu.VMEM)
SMEM = pl.BlockSpec(memory_space=pltpu.SMEM)


def normalize(values):
    widened = values.astype(f32)
    scale = lax.rsqrt(jnp.mean(widened * widened, axis=-1, keepdims=True) + epsilon)
    return (widened * scale).astype(bf16)


def halves(x):
    high = x.astype(bf16)
    return high, (x - high.astype(f32)).astype(bf16)


def nt(a, b):
    return lax.dot_general(a, b, (((1,), (1,)), ((), ())), preferred_element_type=f32)


def nn(a, b):
    return lax.dot_general(a, b, (((1,), (0,)), ((), ())), preferred_element_type=f32)


def tn(a, b):
    return lax.dot_general(a, b, (((0,), (0,)), ((), ())), preferred_element_type=f32)


def project_kernel(whole, wq, wk, wv, wr, query_ref, packed_ref, rates_ref):
    core = lax.axis_index("core")
    chip = (lax.axis_index("xh") * 4 + lax.axis_index("y")) * 8 + lax.axis_index("z")
    left = jnp.concatenate(
        (whole[:TOK_DEV], whole[GATHERED : GATHERED + TOK_DEV]), 0
    )
    base = 2 * GATHERED
    right = jnp.concatenate(
        (whole[base : base + TOK_DEV], whole[base + GATHERED : base + GATHERED + TOK_DEV]), 0
    )

    def both(w):
        return nn(left, w[:FH]) + nn(right, w[FH:])

    def own(w):
        product = both(w)
        return jnp.where(core == 0, product[:, :DH], product[:, DH:]).astype(bf16)

    query_ref[...] = own(wq)
    packed_ref[:ROWS] = jnp.concatenate((own(wk), own(wv)), 1)
    tags = jnp.concatenate(
        (whole[TOK_DEV:GATHERED, :TOK_DEV], whole[GATHERED + TOK_DEV : base, :TOK_DEV]), 1
    )
    packed_ref[ROWS:] = jnp.concatenate((tags, jnp.zeros((16, FH - ROWS), bf16)), 1)
    both_rates = jax.nn.softplus(nt(left, wr[:, :FH]) + nt(right, wr[:, FH:]))
    rates = jnp.where(core == 0, both_rates[:, :1], both_rates[:, 1:])
    rates_ref[...] = rates * jnp.where(chip < 48, 1.0, 0.0)


def gradient_kernel(packed, rates, gate_ref, up_ref, down_ref, sent_ref):
    core = lax.axis_index("core")
    keys_n = normalize(packed[:ROWS, :DH])
    value = packed[:ROWS, DH:].astype(f32)
    gate = nn(keys_n, gate_ref[core].astype(bf16))
    upward = nn(keys_n, up_ref[core].astype(bf16))
    logistic = jax.nn.sigmoid(gate)
    active = gate * logistic
    product = (active * upward).astype(bf16)
    error = (-rates[...] * value).astype(bf16)
    back = nn(error, down_ref[core].astype(bf16))
    grad_g = (back * upward * logistic * (1.0 + gate * (1.0 - logistic))).astype(bf16)
    grad_u = (back * active).astype(bf16)
    sent_ref[:DH] = tn(keys_n, grad_g).astype(bf16)
    sent_ref[DH : 2 * DH] = tn(keys_n, grad_u).astype(bf16)
    sent_ref[2 * DH :] = tn(error, product).astype(bf16)


def add_kernel(got, sent_ref):
    part = got[0].astype(f32)
    for i in range(1, 8):
        part = part + got[i].astype(f32)
    part = part.astype(bf16)
    for i in range(8):
        sent_ref[i] = part


def attend_kernel(query_ref, *refs):
    pieces, attended_ref, scores_ref = refs[:-2], refs[-2], refs[-1]
    query = query_ref[...]
    numbers = lax.broadcasted_iota(jnp.int32, (TAGS, ROWS), 0).astype(f32)

    def marks(piece):
        return jnp.where(numbers == piece[ROWS : ROWS + 1, :ROWS].astype(f32), 1.0, 0.0).astype(bf16)

    own_marks = marks(pieces[0])
    own_marks = jnp.where(numbers > 0.5, own_marks, jnp.zeros_like(own_marks))
    peak = None
    for p, piece in enumerate(pieces):
        scores = nt(query, piece[:ROWS, :DH]) * DH**-0.5
        scores = jnp.where(tn(own_marks, marks(piece)) > 0.5, scores, masked_score)
        scores_ref[:, p * ROWS : (p + 1) * ROWS] = scores
        high = jnp.max(scores, axis=-1, keepdims=True)
        peak = high if peak is None else jnp.maximum(peak, high)
    mass = None
    for p in range(len(pieces)):
        weights = jnp.exp(scores_ref[:, p * ROWS : (p + 1) * ROWS] - peak)
        scores_ref[:, p * ROWS : (p + 1) * ROWS] = weights
        one = jnp.sum(weights, axis=-1, keepdims=True)
        mass = one if mass is None else mass + one
    inverse = 1.0 / mass
    total = None
    for p, piece in enumerate(pieces):
        weights = (scores_ref[:, p * ROWS : (p + 1) * ROWS] * inverse).astype(bf16)
        one = nn(weights, piece[:ROWS, DH:])
        total = one if total is None else total + one
    attended_ref[...] = total


def fresh_kernel(total_ref, gate_ref, up_ref, down_ref, step_ref, query_ref, attended_ref, mixed_ref):
    core = lax.axis_index("core")
    step = step_ref[core]
    currents = []
    for m in range(3):
        matrix = total_ref[m * DH : (m + 1) * DH].astype(f32)
        length = jnp.sqrt(jnp.sum(matrix * matrix))
        currents.append(matrix / (length + epsilon))
    for _ in range(NS_STEPS):
        squares = []
        for x in currents:
            h, l = halves(x)
            squares.append((h, l, nt(h, h) + (nt(h, l) + nt(l, h))))
        mixers = []
        for h, l, a in squares:
            ah, al = halves(a)
            aa = nn(ah, ah) + (nn(ah, al) + nn(al, ah))
            mixers.append((h, l, newton_b * a + newton_c * aa))
        nexts = []
        for x, (h, l, b) in zip(currents, mixers):
            bh, bl = halves(b)
            nexts.append(newton_a * x + (nn(bh, h) + (nn(bh, l) + nn(bl, h))))
        currents = nexts
    fresh = [
        (master[core] - step * ortho).astype(bf16)
        for master, ortho in zip((gate_ref, up_ref, down_ref), currents)
    ]
    queries_n = normalize(query_ref[...])
    gate = nn(queries_n, fresh[0])
    upward = nn(queries_n, fresh[1])
    product = (gate * jax.nn.sigmoid(gate) * upward).astype(bf16)
    mixed_ref[...] = (attended_ref[...] + nt(product, fresh[2])).astype(bf16)


def out_kernel(spread, weight, other, out_ref):
    core = lax.axis_index("core")
    xl = lax.axis_index("xl")
    rows = pl.ds(pl.multiple_of(core * TOK_DEV, TOK_DEV), TOK_DEV)
    columns = pl.ds(pl.multiple_of(xl * FH, FH), FH)
    total = nn(spread[2 * xl, rows], weight[:DH, columns])
    total += nn(spread[2 * xl + 1, rows], weight[DH:, columns])
    total += nn(spread[2 - 2 * xl, rows], other[:DH])
    total += nn(spread[3 - 2 * xl, rows], other[DH:])
    out_ref[...] = total.astype(bf16)


def call(kernel, shapes, args, specs=None, scratch=(), flops=0, bytes_accessed=0, room=12):
    several = isinstance(shapes, (list, tuple))
    return pl.pallas_call(
        kernel,
        out_shape=shapes,
        in_specs=specs or [VMEM] * len(args),
        out_specs=[VMEM] * len(shapes) if several else VMEM,
        scratch_shapes=list(scratch),
        cost_estimate=pl.CostEstimate(
            flops=flops, bytes_accessed=bytes_accessed, transcendentals=0
        ),
        compiler_params=pltpu.CompilerParams(vmem_limit_bytes=room << 20),
    )(*args)


def shape(dims, dtype):
    return jax.ShapeDtypeStruct(dims, dtype)


def hop(x, steps):
    return lax.ppermute(
        x, CHIPS, [(i, i + steps) for i in range(64) if 0 <= i + steps < 64]
    )


def layer(
    tokens,
    view_ids,
    query_weight,
    key_weight,
    value_weight,
    out_weight,
    rate_weight,
    fast_gate,
    fast_up,
    fast_down,
    step_size,
):
    xl = lax.axis_index("xl")
    tag = jnp.pad((view_ids + 1).astype(bf16)[None], ((0, 15), (0, FH - TOK_DEV)))
    whole = lax.all_gather(
        jnp.concatenate((tokens, tag), 0), ("xl", "core"), axis=0, tiled=True
    )
    query, packed, rates = call(
        project_kernel,
        [shape((ROWS, DH), bf16), shape((PACKED, FH), bf16), shape((ROWS, 1), f32)],
        (whole, query_weight, key_weight, value_weight, rate_weight.T),
        flops=2 * 256 * 768 * 1152,
        bytes_accessed=3 << 20,
    )
    pieces = [packed]
    ahead = behind = packed
    for _ in range(REACH):
        ahead = hop(ahead, 1)
        behind = hop(behind, -1)
        pieces += [ahead, behind]

    sent = call(
        gradient_kernel,
        shape((3 * DH, FH), bf16),
        (packed, rates, fast_gate, fast_up, fast_down),
        flops=2 * 256 * 192 * 384 * 6,
        bytes_accessed=3 << 20,
    ).reshape(8, 72, FH)

    def add(got):
        return call(add_kernel, shape((8, 72, FH), bf16), (got,), bytes_accessed=1 << 20)

    got = lax.all_to_all(sent, ("xh", "y"), 0, 0, tiled=True)
    sent = add(got)
    got = lax.all_to_all(sent, "z", 0, 0, tiled=True)
    sent = add(got)
    total = lax.all_to_all(sent, ("xh", "y"), 0, 0, tiled=True)
    total = total.reshape(3 * DH, FH)

    attended = call(
        attend_kernel,
        shape((ROWS, DH), f32),
        (query, *pieces),
        scratch=[pltpu.VMEM((ROWS, len(pieces) * ROWS), f32)],
        flops=4 * 256 * 2304 * 256,
        bytes_accessed=3 << 20,
    )
    mixed = call(
        fresh_kernel,
        shape((ROWS, DH), bf16),
        (total, fast_gate, fast_up, fast_down, step_size, query, attended),
        specs=[VMEM] * 4 + [SMEM] + [VMEM] * 2,
        flops=10**10,
        bytes_accessed=3 << 20,
    )

    theirs = lax.dynamic_slice_in_dim(out_weight, (1 - xl) * FH, FH, 1)
    other = lax.ppermute(theirs, "xl", [(0, 1), (1, 0)])
    spread = lax.all_gather(mixed, ("xl", "core"), axis=0)
    return call(
        out_kernel,
        shape((TOK_DEV, FH), bf16),
        (spread, out_weight, other),
        flops=2 * 128 * 768 * 384,
        bytes_accessed=2 << 20,
    )


def solution(mesh):
    fine = Mesh(mesh.devices.reshape(2, 4, 8, 2, 2), ("xh", "y", "z", "core", "xl"))
    placed = (
        P(TOK, "xl"),
        P(TOK),
        P(None, "xl"),
        P(None, "xl"),
        P(None, "xl"),
        P("xl", None),
        P(None, "xl"),
        P("xl", None, None),
        P("xl", None, None),
        P("xl", None, None),
        P("xl"),
    )
    return jax.shard_map(
        layer, mesh=fine, in_specs=placed, out_specs=P(TOK, "xl"), check_vma=False
    )
```

```python
import jax
import jax.numpy as jnp
from jax import lax
from jax.experimental import pallas as pl
from jax.experimental.pallas import tpu as pltpu
from jax.sharding import Mesh, PartitionSpec as P


NS_STEPS = 5
newton_a = 3.4445
newton_b = -4.775
newton_c = 2.0315
epsilon = 1e-06
masked_score = -1e30

TOK = ("xh", "y", "z", "core")
REACH = 4
DH = 192
FH = 384
TOK_DEV = 128
ROWS = 2 * TOK_DEV
PACKED = ROWS + 16
GATHERED = TOK_DEV + 16
TAGS = 32
f32 = jnp.float32
bf16 = jnp.bfloat16
ANY = pl.BlockSpec(memory_space=pl.ANY)
HBM = pl.BlockSpec(memory_space=pltpu.HBM)
VMEM = pl.BlockSpec(memory_space=pltpu.VMEM)
SMEM = pl.BlockSpec(memory_space=pltpu.SMEM)


def normalize(values):
    widened = values.astype(f32)
    scale = lax.rsqrt(jnp.mean(widened * widened, axis=-1, keepdims=True) + epsilon)
    return (widened * scale).astype(bf16)


def halves(x):
    high = x.astype(bf16)
    return high, (x - high.astype(f32)).astype(bf16)


def nt(a, b):
    return lax.dot_general(a, b, (((1,), (1,)), ((), ())), preferred_element_type=f32)


def nn(a, b):
    return lax.dot_general(a, b, (((1,), (0,)), ((), ())), preferred_element_type=f32)


def tn(a, b):
    return lax.dot_general(a, b, (((0,), (0,)), ((), ())), preferred_element_type=f32)


def copies(sem, *pairs):
    started = [
        pltpu.make_async_copy(source, target, sem.at[i]) for i, (source, target) in enumerate(pairs)
    ]
    for copy in started:
        copy.start()
    return started


def tag_kernel(tokens, views_hbm, tagged_ref, views, sem):
    fetches = copies(sem, (views_hbm, views), (tokens, tagged_ref.at[pl.ds(0, TOK_DEV)]))
    fetches[0].wait()
    row = (views[...] + 1).astype(f32).astype(bf16)
    row = jnp.concatenate((row, jnp.zeros((1, FH - TOK_DEV), bf16)), 1)
    tagged_ref[TOK_DEV:] = jnp.broadcast_to(row, (16, FH))
    fetches[1].wait()


def project_kernel(
    whole, wq_hbm, wk_hbm, wv_hbm, wr, query_hbm, packed_ref, rates_ref, wq, wk, wv, query_ref, sem
):
    fetches = copies(sem, (wq_hbm, wq), (wk_hbm, wk), (wv_hbm, wv))
    core = lax.axis_index("core")
    chip = (lax.axis_index("xh") * 4 + lax.axis_index("y")) * 8 + lax.axis_index("z")
    left = jnp.concatenate(
        (whole[:TOK_DEV], whole[GATHERED : GATHERED + TOK_DEV]), 0
    )
    base = 2 * GATHERED
    right = jnp.concatenate(
        (whole[base : base + TOK_DEV], whole[base + GATHERED : base + GATHERED + TOK_DEV]), 0
    )
    both_rates = jax.nn.softplus(nt(left, wr[:, :FH]) + nt(right, wr[:, FH:]))
    rates = jnp.where(core == 0, both_rates[:, :1], both_rates[:, 1:])
    rates_ref[...] = rates * jnp.where(chip < 48, 1.0, 0.0)
    tags = jnp.concatenate(
        (whole[TOK_DEV:GATHERED, :TOK_DEV], whole[GATHERED + TOK_DEV : base, :TOK_DEV]), 1
    )
    tags = jnp.concatenate((tags, jnp.zeros((16, FH - ROWS), bf16)), 1)

    def both(w):
        return nn(left, w[:FH]) + nn(right, w[FH:])

    fetches[0].wait()
    query = both(wq)
    query_ref[...] = jnp.where(core == 0, query[:, :DH], query[:, DH:]).astype(bf16)
    store = pltpu.make_async_copy(query_ref, query_hbm, sem.at[3])
    store.start()
    fetches[1].wait()
    key = both(wk).astype(bf16)
    fetches[2].wait()
    value = both(wv).astype(bf16)
    for h in range(2):
        part = slice(h * DH, (h + 1) * DH)
        packed_ref[h, :ROWS] = jnp.concatenate((key[:, part], value[:, part]), 1)
        packed_ref[h, ROWS:] = tags
    store.wait()


def gradient_kernel(packed, rates, gate_ref, up_ref, down_ref, sent_ref):
    core = lax.axis_index("core")
    mine = packed[core]
    keys_n = normalize(mine[:ROWS, :DH])
    value = mine[:ROWS, DH:].astype(f32)
    gate = nn(keys_n, gate_ref[core].astype(bf16))
    upward = nn(keys_n, up_ref[core].astype(bf16))
    logistic = jax.nn.sigmoid(gate)
    active = gate * logistic
    product = (active * upward).astype(bf16)
    error = (-rates[...] * value).astype(bf16)
    back = nn(error, down_ref[core].astype(bf16))
    grad_g = (back * upward * logistic * (1.0 + gate * (1.0 - logistic))).astype(bf16)
    grad_u = (back * active).astype(bf16)
    sent_ref[:DH] = tn(keys_n, grad_g).astype(bf16)
    sent_ref[DH : 2 * DH] = tn(keys_n, grad_u).astype(bf16)
    sent_ref[2 * DH :] = tn(error, product).astype(bf16)


def pick_kernel(*refs):
    pieces, picked_ref = refs[:-1], refs[-1]
    core = lax.axis_index("core")
    for i, piece in enumerate(pieces):
        picked_ref[i] = piece[1 - core]


def add_kernel(got, sent_ref):
    part = got[0].astype(f32)
    for i in range(1, 8):
        part = part + got[i].astype(f32)
    part = part.astype(bf16)
    for i in range(8):
        sent_ref[i] = part


def attend_kernel(query_ref, own, *refs):
    relayed, swapped = refs[:REACH], refs[REACH]
    attended_hbm, scores_ref, attended_ref, sem = refs[REACH + 1 :]
    core = lax.axis_index("core")
    query = query_ref[...]
    numbers = lax.broadcasted_iota(jnp.int32, (TAGS, ROWS), 0).astype(f32)
    pieces = [ref.at[core] for ref in (own, *relayed)]
    pieces += [swapped.at[i] for i in range(REACH)]

    def marks(piece):
        return jnp.where(numbers == piece[ROWS : ROWS + 1, :ROWS].astype(f32), 1.0, 0.0).astype(bf16)

    own_marks = marks(pieces[0])
    own_marks = jnp.where(numbers > 0.5, own_marks, jnp.zeros_like(own_marks))
    peak = None
    for p, piece in enumerate(pieces):
        scores = nt(query, piece[:ROWS, :DH]) * DH**-0.5
        scores = jnp.where(tn(own_marks, marks(piece)) > 0.5, scores, masked_score)
        scores_ref[:, p * ROWS : (p + 1) * ROWS] = scores
        high = jnp.max(scores, axis=-1, keepdims=True)
        peak = high if peak is None else jnp.maximum(peak, high)
    mass = None
    for p in range(len(pieces)):
        weights = jnp.exp(scores_ref[:, p * ROWS : (p + 1) * ROWS] - peak)
        scores_ref[:, p * ROWS : (p + 1) * ROWS] = weights
        one = jnp.sum(weights, axis=-1, keepdims=True)
        mass = one if mass is None else mass + one
    inverse = 1.0 / mass
    total = None
    for p, piece in enumerate(pieces):
        weights = (scores_ref[:, p * ROWS : (p + 1) * ROWS] * inverse).astype(bf16)
        one = nn(weights, piece[:ROWS, DH:])
        total = one if total is None else total + one
    attended_ref[...] = total
    store = pltpu.make_async_copy(attended_ref, attended_hbm, sem.at[0])
    store.start()
    store.wait()


def fresh_kernel(
    total_ref, gate_hbm, up_hbm, down_hbm, step_hbm, query_hbm, attended_hbm,
    mixed_ref, masters, step_ref, query_ref, attended_ref, sem,
):
    core = lax.axis_index("core")
    fetches = copies(
        sem,
        (gate_hbm.at[core], masters.at[0]),
        (up_hbm.at[core], masters.at[1]),
        (down_hbm.at[core], masters.at[2]),
        (step_hbm, step_ref),
        (query_hbm, query_ref),
        (attended_hbm, attended_ref),
    )
    currents = []
    for m in range(3):
        matrix = total_ref[m * DH : (m + 1) * DH].astype(f32)
        length = jnp.sqrt(jnp.sum(matrix * matrix))
        currents.append(matrix / (length + epsilon))
    for _ in range(NS_STEPS):
        squares = []
        for x in currents:
            h, l = halves(x)
            cross = nt(h, l)
            squares.append((h, l, nt(h, h) + (cross + cross.T)))
        mixers = []
        for h, l, a in squares:
            ah, al = halves(a)
            cross = nt(ah, al)
            aa = nt(ah, ah) + (cross + cross.T)
            mixers.append((h, l, newton_b * a + newton_c * aa))
        nexts = []
        for x, (h, l, b) in zip(currents, mixers):
            bh, bl = halves(b)
            wide = nn(bh, jnp.concatenate((h, l), 1))
            nexts.append(newton_a * x + (wide[:, :FH] + (wide[:, FH:] + nn(bl, h))))
        currents = nexts
    for fetch in fetches:
        fetch.wait()
    step = step_ref[core]
    fresh = [(masters[m] - step * currents[m]).astype(bf16) for m in range(3)]
    queries_n = normalize(query_ref[...])
    gate = nn(queries_n, fresh[0])
    upward = nn(queries_n, fresh[1])
    product = (gate * jax.nn.sigmoid(gate) * upward).astype(bf16)
    mixed_ref[...] = (attended_ref[...] + nt(product, fresh[2])).astype(bf16)


def out_kernel(spread, weight, other, out_ref):
    core = lax.axis_index("core")
    xl = lax.axis_index("xl")
    rows = pl.ds(pl.multiple_of(core * TOK_DEV, TOK_DEV), TOK_DEV)
    columns = pl.ds(pl.multiple_of(xl * FH, FH), FH)
    total = nn(spread[2 * xl, rows], weight[:DH, columns])
    total += nn(spread[2 * xl + 1, rows], weight[DH:, columns])
    total += nn(spread[2 - 2 * xl, rows], other[:DH])
    total += nn(spread[3 - 2 * xl, rows], other[DH:])
    out_ref[...] = total.astype(bf16)


def call(kernel, shapes, args, specs=None, outs=None, scratch=(), flops=0, bytes_accessed=0, room=12):
    several = isinstance(shapes, (list, tuple))
    args = [
        pltpu.with_memory_space_constraint(arg, pltpu.HBM) if spec is HBM else arg
        for arg, spec in zip(args, specs or [VMEM] * len(args))
    ]
    return pl.pallas_call(
        kernel,
        out_shape=shapes,
        in_specs=specs or [VMEM] * len(args),
        out_specs=outs or ([VMEM] * len(shapes) if several else VMEM),
        scratch_shapes=list(scratch),
        cost_estimate=pl.CostEstimate(
            flops=flops, bytes_accessed=bytes_accessed, transcendentals=0
        ),
        compiler_params=pltpu.CompilerParams(vmem_limit_bytes=room << 20),
    )(*args)


def shape(dims, dtype):
    return jax.ShapeDtypeStruct(dims, dtype)


def hop(x):
    pairs = [(2 * c, 2 * c + 2) for c in range(63)] + [(2 * c + 3, 2 * c + 1) for c in range(63)]
    return lax.ppermute(x, TOK, pairs)


def layer(
    tokens,
    view_ids,
    query_weight,
    key_weight,
    value_weight,
    out_weight,
    rate_weight,
    fast_gate,
    fast_up,
    fast_down,
    step_size,
):
    xl = lax.axis_index("xl")
    tagged = call(
        tag_kernel,
        shape((GATHERED, FH), bf16),
        (tokens, view_ids.reshape(1, TOK_DEV)),
        specs=[HBM, HBM],
        scratch=[pltpu.VMEM((1, TOK_DEV), jnp.int32), pltpu.SemaphoreType.DMA((2,))],
        bytes_accessed=1 << 18,
    )
    whole = lax.all_gather(tagged, ("xl", "core"), axis=0, tiled=True)
    query, packed, rates = call(
        project_kernel,
        [shape((ROWS, DH), bf16), shape((2, PACKED, FH), bf16), shape((ROWS, 1), f32)],
        (whole, query_weight, key_weight, value_weight, rate_weight.T),
        specs=[VMEM, HBM, HBM, HBM, VMEM],
        outs=[ANY, VMEM, VMEM],
        scratch=[pltpu.VMEM((768, FH), bf16)] * 3
        + [pltpu.VMEM((ROWS, DH), bf16), pltpu.SemaphoreType.DMA((4,))],
        flops=2 * 256 * 768 * 1152,
        bytes_accessed=3 << 20,
    )
    relayed = []
    moving = packed
    for _ in range(REACH):
        moving = hop(moving)
        relayed.append(moving)

    sent = call(
        gradient_kernel,
        shape((3 * DH, FH), bf16),
        (packed, rates, fast_gate, fast_up, fast_down),
        flops=2 * 256 * 192 * 384 * 6,
        bytes_accessed=3 << 20,
    ).reshape(8, 72, FH)

    def add(got):
        return call(add_kernel, shape((8, 72, FH), bf16), (got,), bytes_accessed=1 << 20)

    got = lax.all_to_all(sent, ("xh", "y"), 0, 0, tiled=True)
    sent = add(got)
    got = lax.all_to_all(sent, "z", 0, 0, tiled=True)
    sent = add(got)
    total = lax.all_to_all(sent, ("xh", "y"), 0, 0, tiled=True)
    total = total.reshape(3 * DH, FH)

    picked = call(pick_kernel, shape((REACH, PACKED, FH), bf16), relayed, bytes_accessed=2 << 20)
    swapped = lax.ppermute(picked, "core", [(0, 1), (1, 0)])
    attended = call(
        attend_kernel,
        pltpu.HBM((ROWS, DH), f32),
        (query, packed, *relayed, swapped),
        outs=HBM,
        scratch=[
            pltpu.VMEM((ROWS, (2 * REACH + 1) * ROWS), f32),
            pltpu.VMEM((ROWS, DH), f32),
            pltpu.SemaphoreType.DMA((1,)),
        ],
        flops=4 * 256 * 2304 * 256,
        bytes_accessed=3 << 20,
    )
    mixed = call(
        fresh_kernel,
        shape((ROWS, DH), bf16),
        (total, fast_gate, fast_up, fast_down, step_size, query, attended),
        specs=[VMEM] + [HBM] * 4 + [ANY, HBM],
        scratch=[
            pltpu.VMEM((3, DH, FH), f32),
            pltpu.SMEM((2,), f32),
            pltpu.VMEM((ROWS, DH), bf16),
            pltpu.VMEM((ROWS, DH), f32),
            pltpu.SemaphoreType.DMA((6,)),
        ],
        flops=10**10,
        bytes_accessed=3 << 20,
    )

    theirs = lax.dynamic_slice_in_dim(out_weight, (1 - xl) * FH, FH, 1)
    other = lax.ppermute(theirs, "xl", [(0, 1), (1, 0)])
    spread = lax.all_gather(mixed, ("xl", "core"), axis=0)
    return call(
        out_kernel,
        shape((TOK_DEV, FH), bf16),
        (spread, out_weight, other),
        flops=2 * 128 * 768 * 384,
        bytes_accessed=2 << 20,
    )


def solution(mesh):
    fine = Mesh(mesh.devices.reshape(2, 4, 8, 2, 2), ("xh", "y", "z", "core", "xl"))
    placed = (
        P(TOK, "xl"),
        P(TOK),
        P(None, "xl"),
        P(None, "xl"),
        P(None, "xl"),
        P("xl", None),
        P(None, "xl"),
        P("xl", None, None),
        P("xl", None, None),
        P("xl", None, None),
        P("xl"),
    )
    return jax.shard_map(layer, mesh=fine, in_specs=placed, out_specs=P(TOK, "xl"), check_vma=False)
```

```python
import jax
import jax.numpy as jnp
from jax import lax
from jax.experimental import pallas as pl
from jax.experimental.pallas import tpu as pltpu
from jax.sharding import Mesh, PartitionSpec as P


NS_STEPS = 5
newton_a = 3.4445
newton_b = -4.775
newton_c = 2.0315
epsilon = 1e-06
masked_score = -1e30

TOK = ("xh", "y", "z", "core")
CHIPS = ("xh", "y", "z")
REACH = 4
DH = 192
FH = 384
TOK_DEV = 128
ROWS = 2 * TOK_DEV
PACKED = ROWS + 16
GATHERED = TOK_DEV + 16
TAGS = 32
f32 = jnp.float32
bf16 = jnp.bfloat16
ANY = pl.BlockSpec(memory_space=pl.ANY)
HBM = pl.BlockSpec(memory_space=pltpu.HBM)
VMEM = pl.BlockSpec(memory_space=pltpu.VMEM)
SMEM = pl.BlockSpec(memory_space=pltpu.SMEM)


def normalize(values):
    widened = values.astype(f32)
    scale = lax.rsqrt(jnp.mean(widened * widened, axis=-1, keepdims=True) + epsilon)
    return (widened * scale).astype(bf16)


def halves(x):
    high = x.astype(bf16)
    return high, (x - high.astype(f32)).astype(bf16)


def nt(a, b):
    return lax.dot_general(a, b, (((1,), (1,)), ((), ())), preferred_element_type=f32)


def nn(a, b):
    return lax.dot_general(a, b, (((1,), (0,)), ((), ())), preferred_element_type=f32)


def tn(a, b):
    return lax.dot_general(a, b, (((0,), (0,)), ((), ())), preferred_element_type=f32)


def copies(sem, *pairs):
    started = [
        pltpu.make_async_copy(source, target, sem.at[i]) for i, (source, target) in enumerate(pairs)
    ]
    for copy in started:
        copy.start()
    return started


def tag_kernel(tokens, views_hbm, wq_hbm, wk_hbm, wv_hbm, tagged_ref, wq, wk, wv, views, sem):
    fetches = copies(
        sem,
        (views_hbm, views),
        (tokens, tagged_ref.at[pl.ds(0, TOK_DEV)]),
        (wq_hbm, wq),
        (wk_hbm, wk),
        (wv_hbm, wv),
    )
    fetches[0].wait()
    row = (views[...] + 1).astype(f32).astype(bf16)
    row = jnp.concatenate((row, jnp.zeros((1, FH - TOK_DEV), bf16)), 1)
    tagged_ref[TOK_DEV:] = jnp.broadcast_to(row, (16, FH))
    for fetch in fetches[1:]:
        fetch.wait()


def project_kernel(whole, wq, wk, wv, wr, query_ref, packed_ref, rates_ref):
    core = lax.axis_index("core")
    chip = (lax.axis_index("xh") * 4 + lax.axis_index("y")) * 8 + lax.axis_index("z")
    left = jnp.concatenate(
        (whole[:TOK_DEV], whole[GATHERED : GATHERED + TOK_DEV]), 0
    )
    base = 2 * GATHERED
    right = jnp.concatenate(
        (whole[base : base + TOK_DEV], whole[base + GATHERED : base + GATHERED + TOK_DEV]), 0
    )
    both_rates = jax.nn.softplus(nt(left, wr[:, :FH]) + nt(right, wr[:, FH:]))
    rates = jnp.where(core == 0, both_rates[:, :1], both_rates[:, 1:])
    rates_ref[...] = rates * jnp.where(chip < 48, 1.0, 0.0)
    tags = jnp.concatenate(
        (whole[TOK_DEV:GATHERED, :TOK_DEV], whole[GATHERED + TOK_DEV : base, :TOK_DEV]), 1
    )
    tags = jnp.concatenate((tags, jnp.zeros((16, FH - ROWS), bf16)), 1)

    def both(w):
        return nn(left, w[:FH]) + nn(right, w[FH:])

    def own(w):
        product = both(w)
        return jnp.where(core == 0, product[:, :DH], product[:, DH:]).astype(bf16)

    packed_ref[:ROWS] = jnp.concatenate((own(wk), own(wv)), 1)
    packed_ref[ROWS:] = tags
    query_ref[...] = own(wq)


def gradient_kernel(packed, rates, gate_ref, up_ref, down_ref, sent_ref):
    core = lax.axis_index("core")
    keys_n = normalize(packed[:ROWS, :DH])
    value = packed[:ROWS, DH:].astype(f32)
    gate = nn(keys_n, gate_ref[core].astype(bf16))
    upward = nn(keys_n, up_ref[core].astype(bf16))
    logistic = jax.nn.sigmoid(gate)
    active = gate * logistic
    product = (active * upward).astype(bf16)
    error = (-rates[...] * value).astype(bf16)
    back = nn(error, down_ref[core].astype(bf16))
    grad_g = (back * upward * logistic * (1.0 + gate * (1.0 - logistic))).astype(bf16)
    grad_u = (back * active).astype(bf16)
    sent_ref[:DH] = tn(keys_n, grad_g).astype(bf16)
    sent_ref[DH : 2 * DH] = tn(keys_n, grad_u).astype(bf16)
    sent_ref[2 * DH :] = tn(error, product).astype(bf16)


def add_kernel(got, sent_ref):
    part = got[0].astype(f32)
    for i in range(1, 8):
        part = part + got[i].astype(f32)
    part = part.astype(bf16)
    for i in range(8):
        sent_ref[i] = part


def blend_kernel(query_ref, fresh, *refs):
    pieces, mixed_ref, scores_ref = refs[: 2 * REACH + 1], refs[-2], refs[-1]
    query = query_ref[...]
    numbers = lax.broadcasted_iota(jnp.int32, (TAGS, ROWS), 0).astype(f32)

    def marks(piece):
        return jnp.where(numbers == piece[ROWS : ROWS + 1, :ROWS].astype(f32), 1.0, 0.0).astype(bf16)

    own_marks = marks(pieces[0])
    own_marks = jnp.where(numbers > 0.5, own_marks, jnp.zeros_like(own_marks))
    peak = None
    for p, piece in enumerate(pieces):
        scores = nt(query, piece[:ROWS, :DH]) * DH**-0.5
        scores = jnp.where(tn(own_marks, marks(piece)) > 0.5, scores, masked_score)
        scores_ref[:, p * ROWS : (p + 1) * ROWS] = scores
        high = jnp.max(scores, axis=-1, keepdims=True)
        peak = high if peak is None else jnp.maximum(peak, high)
    mass = None
    for p in range(len(pieces)):
        weights = jnp.exp(scores_ref[:, p * ROWS : (p + 1) * ROWS] - peak)
        scores_ref[:, p * ROWS : (p + 1) * ROWS] = weights
        one = jnp.sum(weights, axis=-1, keepdims=True)
        mass = one if mass is None else mass + one
    inverse = 1.0 / mass
    total = None
    for p, piece in enumerate(pieces):
        weights = (scores_ref[:, p * ROWS : (p + 1) * ROWS] * inverse).astype(bf16)
        one = nn(weights, piece[:ROWS, DH:])
        total = one if total is None else total + one
    queries_n = normalize(query)
    gate = nn(queries_n, fresh[0])
    upward = nn(queries_n, fresh[1])
    product = (gate * jax.nn.sigmoid(gate) * upward).astype(bf16)
    mixed_ref[...] = (total + nt(product, fresh[2])).astype(bf16)


def fresh_kernel(total_ref, gate_hbm, up_hbm, down_hbm, step_hbm, fresh_ref, masters, step_ref, sem):
    core = lax.axis_index("core")
    fetches = copies(
        sem,
        (gate_hbm.at[core], masters.at[0]),
        (up_hbm.at[core], masters.at[1]),
        (down_hbm.at[core], masters.at[2]),
        (step_hbm, step_ref),
    )
    currents = []
    for m in range(3):
        matrix = total_ref[m * DH : (m + 1) * DH].astype(f32)
        length = jnp.sqrt(jnp.sum(matrix * matrix))
        currents.append(matrix / (length + epsilon))
    for _ in range(NS_STEPS):
        squares = []
        for x in currents:
            h, l = halves(x)
            cross = nt(h, l)
            squares.append((h, l, nt(h, h) + (cross + cross.T)))
        mixers = []
        for h, l, a in squares:
            ah, al = halves(a)
            cross = nt(ah, al)
            aa = nt(ah, ah) + (cross + cross.T)
            mixers.append((h, l, newton_b * a + newton_c * aa))
        nexts = []
        for x, (h, l, b) in zip(currents, mixers):
            bh, bl = halves(b)
            wide = nn(bh, jnp.concatenate((h, l), 1))
            nexts.append(newton_a * x + (wide[:, :FH] + (wide[:, FH:] + nn(bl, h))))
        currents = nexts
    for fetch in fetches:
        fetch.wait()
    step = step_ref[core]
    for m in range(3):
        fresh_ref[m] = (masters[m] - step * currents[m]).astype(bf16)


def out_kernel(spread, weight, other, out_ref):
    core = lax.axis_index("core")
    xl = lax.axis_index("xl")
    rows = pl.ds(pl.multiple_of(core * TOK_DEV, TOK_DEV), TOK_DEV)
    columns = pl.ds(pl.multiple_of(xl * FH, FH), FH)
    total = nn(spread[2 * xl, rows], weight[:DH, columns])
    total += nn(spread[2 * xl + 1, rows], weight[DH:, columns])
    total += nn(spread[2 - 2 * xl, rows], other[:DH])
    total += nn(spread[3 - 2 * xl, rows], other[DH:])
    out_ref[...] = total.astype(bf16)


def call(kernel, shapes, args, specs=None, outs=None, scratch=(), flops=0, bytes_accessed=0, room=12):
    several = isinstance(shapes, (list, tuple))
    args = [
        pltpu.with_memory_space_constraint(arg, pltpu.HBM) if spec is HBM else arg
        for arg, spec in zip(args, specs or [VMEM] * len(args))
    ]
    return pl.pallas_call(
        kernel,
        out_shape=shapes,
        in_specs=specs or [VMEM] * len(args),
        out_specs=outs or ([VMEM] * len(shapes) if several else VMEM),
        scratch_shapes=list(scratch),
        cost_estimate=pl.CostEstimate(
            flops=flops, bytes_accessed=bytes_accessed, transcendentals=0
        ),
        compiler_params=pltpu.CompilerParams(vmem_limit_bytes=room << 20),
    )(*args)


def shape(dims, dtype):
    return jax.ShapeDtypeStruct(dims, dtype)


def hop(x, steps):
    return lax.ppermute(
        x, CHIPS, [(i, i + steps) for i in range(64) if 0 <= i + steps < 64]
    )


def layer(
    tokens,
    view_ids,
    query_weight,
    key_weight,
    value_weight,
    out_weight,
    rate_weight,
    fast_gate,
    fast_up,
    fast_down,
    step_size,
):
    xl = lax.axis_index("xl")
    tagged, *weights = call(
        tag_kernel,
        [shape((GATHERED, FH), bf16)] + [shape((768, FH), bf16)] * 3,
        (tokens, view_ids.reshape(1, TOK_DEV), query_weight, key_weight, value_weight),
        specs=[HBM] * 5,
        scratch=[pltpu.VMEM((1, TOK_DEV), jnp.int32), pltpu.SemaphoreType.DMA((5,))],
        bytes_accessed=1 << 18,
    )
    whole = lax.all_gather(tagged, ("xl", "core"), axis=0, tiled=True)
    query, packed, rates = call(
        project_kernel,
        [shape((ROWS, DH), bf16), shape((PACKED, FH), bf16), shape((ROWS, 1), f32)],
        (whole, *weights, rate_weight.T),
        flops=2 * 256 * 768 * 1152,
        bytes_accessed=3 << 20,
    )
    pieces = [packed]
    ahead = behind = packed
    for _ in range(REACH):
        ahead = hop(ahead, 1)
        behind = hop(behind, -1)
        pieces += [ahead, behind]

    sent = call(
        gradient_kernel,
        shape((3 * DH, FH), bf16),
        (packed, rates, fast_gate, fast_up, fast_down),
        flops=2 * 256 * 192 * 384 * 6,
        bytes_accessed=3 << 20,
    ).reshape(8, 72, FH)

    def add(got):
        return call(add_kernel, shape((8, 72, FH), bf16), (got,), bytes_accessed=1 << 20)

    got = lax.all_to_all(sent, ("xh", "y"), 0, 0, tiled=True)
    sent = add(got)
    got = lax.all_to_all(sent, "z", 0, 0, tiled=True)
    sent = add(got)
    total = lax.all_to_all(sent, ("xh", "y"), 0, 0, tiled=True)
    total = total.reshape(3 * DH, FH)

    fresh = call(
        fresh_kernel,
        shape((3, DH, FH), bf16),
        (total, fast_gate, fast_up, fast_down, step_size),
        specs=[VMEM] + [HBM] * 4,
        scratch=[
            pltpu.VMEM((3, DH, FH), f32),
            pltpu.SMEM((2,), f32),
            pltpu.SemaphoreType.DMA((4,)),
        ],
        flops=10**10,
        bytes_accessed=3 << 20,
    )
    mixed = call(
        blend_kernel,
        shape((ROWS, DH), bf16),
        (query, fresh, *pieces),
        scratch=[pltpu.VMEM((ROWS, len(pieces) * ROWS), f32)],
        flops=4 * 256 * 2304 * 256,
        bytes_accessed=3 << 20,
    )

    theirs = lax.dynamic_slice_in_dim(out_weight, (1 - xl) * FH, FH, 1)
    other = lax.ppermute(theirs, "xl", [(0, 1), (1, 0)])
    spread = lax.all_gather(mixed, ("xl", "core"), axis=0)
    return call(
        out_kernel,
        shape((TOK_DEV, FH), bf16),
        (spread, out_weight, other),
        flops=2 * 128 * 768 * 384,
        bytes_accessed=2 << 20,
    )


def solution(mesh):
    fine = Mesh(mesh.devices.reshape(2, 4, 8, 2, 2), ("xh", "y", "z", "core", "xl"))
    placed = (
        P(TOK, "xl"),
        P(TOK),
        P(None, "xl"),
        P(None, "xl"),
        P(None, "xl"),
        P("xl", None),
        P(None, "xl"),
        P("xl", None, None),
        P("xl", None, None),
        P("xl", None, None),
        P("xl"),
    )
    return jax.shard_map(layer, mesh=fine, in_specs=placed, out_specs=P(TOK, "xl"), check_vma=False)
```

```python
import jax
import jax.numpy as jnp
from jax import lax
from jax.experimental import pallas as pl
from jax.experimental.pallas import tpu as pltpu
from jax.sharding import Mesh, PartitionSpec as P


NS_STEPS = 5
newton_a = 3.4445
newton_b = -4.775
newton_c = 2.0315
epsilon = 1e-06
masked_score = -1e30

TOK = ("xh", "y", "z", "core")
CHIPS = ("xh", "y", "z")
REACH = 4
DH = 192
FH = 384
TOK_DEV = 128
ROWS = 2 * TOK_DEV
PACKED = ROWS + 16
GATHERED = TOK_DEV + 16
TAGS = 32
f32 = jnp.float32
bf16 = jnp.bfloat16
ANY = pl.BlockSpec(memory_space=pl.ANY)
HBM = pl.BlockSpec(memory_space=pltpu.HBM)
VMEM = pl.BlockSpec(memory_space=pltpu.VMEM)
SMEM = pl.BlockSpec(memory_space=pltpu.SMEM)


def normalize(values):
    widened = values.astype(f32)
    scale = lax.rsqrt(jnp.mean(widened * widened, axis=-1, keepdims=True) + epsilon)
    return (widened * scale).astype(bf16)


def halves(x):
    high = x.astype(bf16)
    return high, (x - high.astype(f32)).astype(bf16)


def nt(a, b):
    return lax.dot_general(a, b, (((1,), (1,)), ((), ())), preferred_element_type=f32)


def nn(a, b):
    return lax.dot_general(a, b, (((1,), (0,)), ((), ())), preferred_element_type=f32)


def tn(a, b):
    return lax.dot_general(a, b, (((0,), (0,)), ((), ())), preferred_element_type=f32)


def copies(sem, *pairs):
    started = [
        pltpu.make_async_copy(source, target, sem.at[i]) for i, (source, target) in enumerate(pairs)
    ]
    for copy in started:
        copy.start()
    return started


def tag_kernel(
    tokens, views_hbm, wq_hbm, wk_hbm, wv_hbm, wr_hbm, wo_hbm,
    tagged_ref, wq, wk, wv, wr, theirs, views, sem,
):
    columns = pl.ds(pl.multiple_of((1 - lax.axis_index("xl")) * FH, FH), FH)
    fetches = copies(
        sem,
        (views_hbm, views),
        (tokens, tagged_ref.at[pl.ds(0, TOK_DEV)]),
        (wq_hbm, wq),
        (wk_hbm, wk),
        (wv_hbm, wv),
        (wr_hbm, wr),
        (wo_hbm.at[:, columns], theirs),
    )
    fetches[0].wait()
    row = (views[...] + 1).astype(f32).astype(bf16)
    row = jnp.concatenate((row, jnp.zeros((1, FH - TOK_DEV), bf16)), 1)
    tagged_ref[TOK_DEV:] = jnp.broadcast_to(row, (16, FH))
    for fetch in fetches[1:]:
        fetch.wait()


def project_kernel(whole, wq, wk, wv, wr, query_ref, packed_ref, rates_ref):
    core = lax.axis_index("core")
    chip = (lax.axis_index("xh") * 4 + lax.axis_index("y")) * 8 + lax.axis_index("z")
    left = jnp.concatenate(
        (whole[:TOK_DEV], whole[GATHERED : GATHERED + TOK_DEV]), 0
    )
    base = 2 * GATHERED
    right = jnp.concatenate(
        (whole[base : base + TOK_DEV], whole[base + GATHERED : base + GATHERED + TOK_DEV]), 0
    )
    both_rates = jax.nn.softplus(nt(left, wr[:, :FH]) + nt(right, wr[:, FH:]))
    rates = jnp.where(core == 0, both_rates[:, :1], both_rates[:, 1:])
    rates_ref[...] = rates * jnp.where(chip < 48, 1.0, 0.0)
    tags = jnp.concatenate(
        (whole[TOK_DEV:GATHERED, :TOK_DEV], whole[GATHERED + TOK_DEV : base, :TOK_DEV]), 1
    )
    tags = jnp.concatenate((tags, jnp.zeros((16, FH - ROWS), bf16)), 1)

    def both(w):
        return nn(left, w[:FH]) + nn(right, w[FH:])

    def own(w):
        product = both(w)
        return jnp.where(core == 0, product[:, :DH], product[:, DH:]).astype(bf16)

    packed_ref[:ROWS] = jnp.concatenate((own(wk), own(wv)), 1)
    packed_ref[ROWS:] = tags
    query_ref[...] = own(wq)


def gradient_kernel(packed, rates, gate_ref, up_ref, down_ref, sent_ref):
    core = lax.axis_index("core")
    keys_n = normalize(packed[:ROWS, :DH])
    value = packed[:ROWS, DH:].astype(f32)
    gate = nn(keys_n, gate_ref[core].astype(bf16))
    upward = nn(keys_n, up_ref[core].astype(bf16))
    logistic = jax.nn.sigmoid(gate)
    active = gate * logistic
    product = (active * upward).astype(bf16)
    error = (-rates[...] * value).astype(bf16)
    back = nn(error, down_ref[core].astype(bf16))
    grad_g = (back * upward * logistic * (1.0 + gate * (1.0 - logistic))).astype(bf16)
    grad_u = (back * active).astype(bf16)
    sent_ref[:DH] = tn(keys_n, grad_g).astype(bf16)
    sent_ref[DH : 2 * DH] = tn(keys_n, grad_u).astype(bf16)
    sent_ref[2 * DH :] = tn(error, product).astype(bf16)


def add_kernel(got, sent_ref):
    part = got[0].astype(f32)
    for i in range(1, 8):
        part = part + got[i].astype(f32)
    part = part.astype(bf16)
    for i in range(8):
        sent_ref[i] = part


def blend_kernel(query_ref, fresh, *refs):
    pieces, mixed_ref, scores_ref = refs[: 2 * REACH + 1], refs[-2], refs[-1]
    query = query_ref[...]
    numbers = lax.broadcasted_iota(jnp.int32, (TAGS, ROWS), 0).astype(f32)

    def marks(piece):
        return jnp.where(numbers == piece[ROWS : ROWS + 1, :ROWS].astype(f32), 1.0, 0.0).astype(bf16)

    own_marks = marks(pieces[0])
    own_marks = jnp.where(numbers > 0.5, own_marks, jnp.zeros_like(own_marks))
    peak = None
    for p, piece in enumerate(pieces):
        scores = nt(query, piece[:ROWS, :DH]) * DH**-0.5
        scores = jnp.where(tn(own_marks, marks(piece)) > 0.5, scores, masked_score)
        scores_ref[:, p * ROWS : (p + 1) * ROWS] = scores
        high = jnp.max(scores, axis=-1, keepdims=True)
        peak = high if peak is None else jnp.maximum(peak, high)
    mass = None
    for p in range(len(pieces)):
        weights = jnp.exp(scores_ref[:, p * ROWS : (p + 1) * ROWS] - peak)
        scores_ref[:, p * ROWS : (p + 1) * ROWS] = weights
        one = jnp.sum(weights, axis=-1, keepdims=True)
        mass = one if mass is None else mass + one
    inverse = 1.0 / mass
    total = None
    for p, piece in enumerate(pieces):
        weights = (scores_ref[:, p * ROWS : (p + 1) * ROWS] * inverse).astype(bf16)
        one = nn(weights, piece[:ROWS, DH:])
        total = one if total is None else total + one
    queries_n = normalize(query)
    gate = nn(queries_n, fresh[0])
    upward = nn(queries_n, fresh[1])
    product = (gate * jax.nn.sigmoid(gate) * upward).astype(bf16)
    mixed_ref[...] = (total + nt(product, fresh[2])).astype(bf16)


def fresh_kernel(total_ref, gate_hbm, up_hbm, down_hbm, step_hbm, fresh_ref, masters, step_ref, sem):
    core = lax.axis_index("core")
    fetches = copies(
        sem,
        (gate_hbm.at[core], masters.at[0]),
        (up_hbm.at[core], masters.at[1]),
        (down_hbm.at[core], masters.at[2]),
        (step_hbm, step_ref),
    )
    currents = []
    for m in range(3):
        matrix = total_ref[m * DH : (m + 1) * DH].astype(f32)
        length = jnp.sqrt(jnp.sum(matrix * matrix))
        currents.append(matrix / (length + epsilon))
    for _ in range(NS_STEPS):
        squares = []
        for x in currents:
            h, l = halves(x)
            cross = nt(h, l)
            squares.append((h, l, nt(h, h) + (cross + cross.T)))
        mixers = []
        for h, l, a in squares:
            ah, al = halves(a)
            cross = nt(ah, al)
            aa = nt(ah, ah) + (cross + cross.T)
            mixers.append((h, l, newton_b * a + newton_c * aa))
        nexts = []
        for x, (h, l, b) in zip(currents, mixers):
            bh, bl = halves(b)
            wide = nn(bh, jnp.concatenate((h, l), 1))
            nexts.append(newton_a * x + (wide[:, :FH] + (wide[:, FH:] + nn(bl, h))))
        currents = nexts
    for fetch in fetches:
        fetch.wait()
    step = step_ref[core]
    for m in range(3):
        fresh_ref[m] = (masters[m] - step * currents[m]).astype(bf16)


def out_kernel(spread, weight, other, out_ref):
    core = lax.axis_index("core")
    xl = lax.axis_index("xl")
    rows = pl.ds(pl.multiple_of(core * TOK_DEV, TOK_DEV), TOK_DEV)
    columns = pl.ds(pl.multiple_of(xl * FH, FH), FH)
    total = nn(spread[2 * xl, rows], weight[:DH, columns])
    total += nn(spread[2 * xl + 1, rows], weight[DH:, columns])
    total += nn(spread[2 - 2 * xl, rows], other[:DH])
    total += nn(spread[3 - 2 * xl, rows], other[DH:])
    out_ref[...] = total.astype(bf16)


def call(kernel, shapes, args, specs=None, outs=None, scratch=(), flops=0, bytes_accessed=0, room=12):
    several = isinstance(shapes, (list, tuple))
    args = [
        pltpu.with_memory_space_constraint(arg, pltpu.HBM) if spec is HBM else arg
        for arg, spec in zip(args, specs or [VMEM] * len(args))
    ]
    return pl.pallas_call(
        kernel,
        out_shape=shapes,
        in_specs=specs or [VMEM] * len(args),
        out_specs=outs or ([VMEM] * len(shapes) if several else VMEM),
        scratch_shapes=list(scratch),
        cost_estimate=pl.CostEstimate(
            flops=flops, bytes_accessed=bytes_accessed, transcendentals=0
        ),
        compiler_params=pltpu.CompilerParams(vmem_limit_bytes=room << 20),
    )(*args)


def shape(dims, dtype):
    return jax.ShapeDtypeStruct(dims, dtype)


def hop(x, steps):
    return lax.ppermute(
        x, CHIPS, [(i, i + steps) for i in range(64) if 0 <= i + steps < 64]
    )


def layer(
    tokens,
    view_ids,
    query_weight,
    key_weight,
    value_weight,
    out_weight,
    rate_weight,
    fast_gate,
    fast_up,
    fast_down,
    step_size,
):
    tagged, *weights, theirs = call(
        tag_kernel,
        [shape((GATHERED, FH), bf16)]
        + [shape((768, FH), bf16)] * 3
        + [shape((2, 768), bf16), shape((FH, FH), bf16)],
        (
            tokens,
            view_ids.reshape(1, TOK_DEV),
            query_weight,
            key_weight,
            value_weight,
            rate_weight.T,
            out_weight,
        ),
        specs=[HBM] * 7,
        scratch=[pltpu.VMEM((1, TOK_DEV), jnp.int32), pltpu.SemaphoreType.DMA((7,))],
        bytes_accessed=1 << 18,
    )
    whole = lax.all_gather(tagged, ("xl", "core"), axis=0, tiled=True)
    query, packed, rates = call(
        project_kernel,
        [shape((ROWS, DH), bf16), shape((PACKED, FH), bf16), shape((ROWS, 1), f32)],
        (whole, *weights),
        flops=2 * 256 * 768 * 1152,
        bytes_accessed=3 << 20,
    )
    pieces = [packed]
    ahead = behind = packed
    for _ in range(REACH):
        ahead = hop(ahead, 1)
        behind = hop(behind, -1)
        pieces += [ahead, behind]

    sent = call(
        gradient_kernel,
        shape((3 * DH, FH), bf16),
        (packed, rates, fast_gate, fast_up, fast_down),
        flops=2 * 256 * 192 * 384 * 6,
        bytes_accessed=3 << 20,
    ).reshape(8, 72, FH)

    def add(got):
        return call(add_kernel, shape((8, 72, FH), bf16), (got,), bytes_accessed=1 << 20)

    got = lax.all_to_all(sent, ("xh", "y"), 0, 0, tiled=True)
    sent = add(got)
    got = lax.all_to_all(sent, "z", 0, 0, tiled=True)
    sent = add(got)
    total = lax.all_to_all(sent, ("xh", "y"), 0, 0, tiled=True)
    total = total.reshape(3 * DH, FH)

    fresh = call(
        fresh_kernel,
        shape((3, DH, FH), bf16),
        (total, fast_gate, fast_up, fast_down, step_size),
        specs=[VMEM] + [HBM] * 4,
        scratch=[
            pltpu.VMEM((3, DH, FH), f32),
            pltpu.SMEM((2,), f32),
            pltpu.SemaphoreType.DMA((4,)),
        ],
        flops=10**10,
        bytes_accessed=3 << 20,
    )
    mixed = call(
        blend_kernel,
        shape((ROWS, DH), bf16),
        (query, fresh, *pieces),
        scratch=[pltpu.VMEM((ROWS, len(pieces) * ROWS), f32)],
        flops=4 * 256 * 2304 * 256,
        bytes_accessed=3 << 20,
    )

    other = lax.ppermute(theirs, "xl", [(0, 1), (1, 0)])
    spread = lax.all_gather(mixed, ("xl", "core"), axis=0)
    return call(
        out_kernel,
        shape((TOK_DEV, FH), bf16),
        (spread, out_weight, other),
        flops=2 * 128 * 768 * 384,
        bytes_accessed=2 << 20,
    )


def solution(mesh):
    fine = Mesh(mesh.devices.reshape(2, 4, 8, 2, 2), ("xh", "y", "z", "core", "xl"))
    placed = (
        P(TOK, "xl"),
        P(TOK),
        P(None, "xl"),
        P(None, "xl"),
        P(None, "xl"),
        P("xl", None),
        P(None, "xl"),
        P("xl", None, None),
        P("xl", None, None),
        P("xl", None, None),
        P("xl"),
    )
    return jax.shard_map(
        layer, mesh=fine, in_specs=placed, out_specs=P(TOK, "xl"), check_vma=False
    )
```

```python
import jax
import jax.numpy as jnp
from jax import lax
from jax.experimental import pallas as pl
from jax.experimental.pallas import tpu as pltpu
from jax.sharding import Mesh, PartitionSpec as P


NS_STEPS = 5
newton_a = 3.4445
newton_b = -4.775
newton_c = 2.0315
epsilon = 1e-06
masked_score = -1e30

TOK = ("xh", "y", "z", "core")
CHIPS = ("xh", "y", "z")
REACH = 4
DH = 192
FH = 384
TOK_DEV = 128
ROWS = 2 * TOK_DEV
PACKED = ROWS + 16
GATHERED = TOK_DEV + 16
TAGS = 32
WIDE = 256
f32 = jnp.float32
bf16 = jnp.bfloat16
ANY = pl.BlockSpec(memory_space=pl.ANY)
HBM = pl.BlockSpec(memory_space=pltpu.HBM)
VMEM = pl.BlockSpec(memory_space=pltpu.VMEM)
SMEM = pl.BlockSpec(memory_space=pltpu.SMEM)


def normalize(values):
    widened = values.astype(f32)
    scale = lax.rsqrt(jnp.mean(widened * widened, axis=-1, keepdims=True) + epsilon)
    return (widened * scale).astype(bf16)


def halves(x):
    high = x.astype(bf16)
    return high, (x - high.astype(f32)).astype(bf16)


def nt(a, b):
    return lax.dot_general(a, b, (((1,), (1,)), ((), ())), preferred_element_type=f32)


def nn(a, b):
    return lax.dot_general(a, b, (((1,), (0,)), ((), ())), preferred_element_type=f32)


def tn(a, b):
    return lax.dot_general(a, b, (((0,), (0,)), ((), ())), preferred_element_type=f32)


def copies(sem, *pairs):
    started = [
        pltpu.make_async_copy(source, target, sem.at[i]) for i, (source, target) in enumerate(pairs)
    ]
    for copy in started:
        copy.start()
    return started


def tag_kernel(
    tokens, views_hbm, wq_hbm, wk_hbm, wv_hbm, wr_hbm, wo_hbm,
    tagged_ref, wq, wk, wv, wr, theirs, views, sem,
):
    columns = pl.ds(pl.multiple_of((1 - lax.axis_index("xl")) * FH, FH), FH)
    near = pl.ds(pl.multiple_of(lax.axis_index("core") * TOK_DEV, TOK_DEV), WIDE)
    fetches = copies(
        sem,
        (views_hbm, views),
        (tokens, tagged_ref.at[pl.ds(0, TOK_DEV)]),
        (wq_hbm.at[:, near], wq),
        (wk_hbm.at[:, near], wk),
        (wv_hbm.at[:, near], wv),
        (wr_hbm, wr),
        (wo_hbm.at[:, columns], theirs),
    )
    fetches[0].wait()
    row = (views[...] + 1).astype(f32).astype(bf16)
    row = jnp.concatenate((row, jnp.zeros((1, FH - TOK_DEV), bf16)), 1)
    tagged_ref[TOK_DEV:] = jnp.broadcast_to(row, (16, FH))
    for fetch in fetches[1:]:
        fetch.wait()


def project_kernel(whole, wq, wk, wv, wr, query_ref, packed_ref, rates_ref):
    core = lax.axis_index("core")
    chip = (lax.axis_index("xh") * 4 + lax.axis_index("y")) * 8 + lax.axis_index("z")
    left = jnp.concatenate(
        (whole[:TOK_DEV], whole[GATHERED : GATHERED + TOK_DEV]), 0
    )
    base = 2 * GATHERED
    right = jnp.concatenate(
        (whole[base : base + TOK_DEV], whole[base + GATHERED : base + GATHERED + TOK_DEV]), 0
    )
    both_rates = jax.nn.softplus(nt(left, wr[:, :FH]) + nt(right, wr[:, FH:]))
    rates = jnp.where(core == 0, both_rates[:, :1], both_rates[:, 1:])
    rates_ref[...] = rates * jnp.where(chip < 48, 1.0, 0.0)
    tags = jnp.concatenate(
        (whole[TOK_DEV:GATHERED, :TOK_DEV], whole[GATHERED + TOK_DEV : base, :TOK_DEV]), 1
    )
    tags = jnp.concatenate((tags, jnp.zeros((16, FH - ROWS), bf16)), 1)

    def both(w):
        return nn(left, w[:FH]) + nn(right, w[FH:])

    def own(w):
        product = both(w)
        return jnp.where(core == 0, product[:, :DH], product[:, WIDE - DH :]).astype(bf16)

    packed_ref[:ROWS] = jnp.concatenate((own(wk), own(wv)), 1)
    packed_ref[ROWS:] = tags
    query_ref[...] = own(wq)


def gradient_kernel(packed, rates, gate_ref, up_ref, down_ref, sent_hbm, sent_ref, sem):
    core = lax.axis_index("core")
    keys_n = normalize(packed[:ROWS, :DH])
    value = packed[:ROWS, DH:].astype(f32)
    gate = nn(keys_n, gate_ref[core].astype(bf16))
    upward = nn(keys_n, up_ref[core].astype(bf16))
    logistic = jax.nn.sigmoid(gate)
    active = gate * logistic
    product = (active * upward).astype(bf16)
    error = (-rates[...] * value).astype(bf16)
    stores = []

    def send(i, part):
        rows = pl.ds(i * DH, DH)
        sent_ref[rows] = part.astype(bf16)
        stores.append(pltpu.make_async_copy(sent_ref.at[rows], sent_hbm.at[rows], sem.at[i]))
        stores[-1].start()

    send(2, tn(error, product))
    back = nn(error, down_ref[core].astype(bf16))
    send(1, tn(keys_n, (back * active).astype(bf16)))
    grad_g = (back * upward * logistic * (1.0 + gate * (1.0 - logistic))).astype(bf16)
    send(0, tn(keys_n, grad_g))
    for store in stores:
        store.wait()


def add_kernel(got, sent_hbm, part_ref, sem):
    part = got[0].astype(f32)
    for i in range(1, 8):
        part = part + got[i].astype(f32)
    part_ref[...] = part.astype(bf16)
    for store in copies(sem, *[(part_ref, sent_hbm.at[i]) for i in range(8)]):
        store.wait()


def blend_kernel(query_ref, fresh, *refs):
    pieces, mixed_ref, scores_ref = refs[: 2 * REACH + 1], refs[-2], refs[-1]
    query = query_ref[...]
    numbers = lax.broadcasted_iota(jnp.int32, (TAGS, ROWS), 0).astype(f32)

    def marks(piece):
        return jnp.where(numbers == piece[ROWS : ROWS + 1, :ROWS].astype(f32), 1.0, 0.0).astype(bf16)

    own_marks = marks(pieces[0])
    own_marks = jnp.where(numbers > 0.5, own_marks, jnp.zeros_like(own_marks))
    peak = None
    for p, piece in enumerate(pieces):
        scores = nt(query, piece[:ROWS, :DH]) * DH**-0.5
        scores = jnp.where(tn(own_marks, marks(piece)) > 0.5, scores, masked_score)
        scores_ref[:, p * ROWS : (p + 1) * ROWS] = scores
        high = jnp.max(scores, axis=-1, keepdims=True)
        peak = high if peak is None else jnp.maximum(peak, high)
    mass = None
    for p in range(len(pieces)):
        weights = jnp.exp(scores_ref[:, p * ROWS : (p + 1) * ROWS] - peak)
        scores_ref[:, p * ROWS : (p + 1) * ROWS] = weights
        one = jnp.sum(weights, axis=-1, keepdims=True)
        mass = one if mass is None else mass + one
    inverse = 1.0 / mass
    total = None
    for p, piece in enumerate(pieces):
        weights = (scores_ref[:, p * ROWS : (p + 1) * ROWS] * inverse).astype(bf16)
        one = nn(weights, piece[:ROWS, DH:])
        total = one if total is None else total + one
    queries_n = normalize(query)
    gate = nn(queries_n, fresh[0])
    upward = nn(queries_n, fresh[1])
    product = (gate * jax.nn.sigmoid(gate) * upward).astype(bf16)
    mixed_ref[...] = (total + nt(product, fresh[2])).astype(bf16)


def fresh_kernel(total_ref, gate_hbm, up_hbm, down_hbm, step_hbm, fresh_ref, masters, step_ref, sem):
    core = lax.axis_index("core")
    fetches = copies(
        sem,
        (gate_hbm.at[core], masters.at[0]),
        (up_hbm.at[core], masters.at[1]),
        (down_hbm.at[core], masters.at[2]),
        (step_hbm, step_ref),
    )
    currents = []
    for m in range(3):
        matrix = total_ref[m * DH : (m + 1) * DH].astype(f32)
        length = jnp.sqrt(jnp.sum(matrix * matrix))
        currents.append(matrix / (length + epsilon))
    for _ in range(NS_STEPS):
        squares = []
        for x in currents:
            h, l = halves(x)
            cross = nt(h, l)
            squares.append((h, l, nt(h, h) + (cross + cross.T)))
        mixers = []
        for h, l, a in squares:
            ah, al = halves(a)
            cross = nt(ah, al)
            aa = nt(ah, ah) + (cross + cross.T)
            mixers.append((h, l, newton_b * a + newton_c * aa))
        nexts = []
        for x, (h, l, b) in zip(currents, mixers):
            bh, bl = halves(b)
            wide = nn(bh, jnp.concatenate((h, l), 1))
            nexts.append(newton_a * x + (wide[:, :FH] + (wide[:, FH:] + nn(bl, h))))
        currents = nexts
    for fetch in fetches:
        fetch.wait()
    step = step_ref[core]
    for m in range(3):
        fresh_ref[m] = (masters[m] - step * currents[m]).astype(bf16)


def out_kernel(spread, weight, other, out_ref):
    core = lax.axis_index("core")
    xl = lax.axis_index("xl")
    rows = pl.ds(pl.multiple_of(core * TOK_DEV, TOK_DEV), TOK_DEV)
    columns = pl.ds(pl.multiple_of(xl * FH, FH), FH)
    total = nn(spread[2 * xl, rows], weight[:DH, columns])
    total += nn(spread[2 * xl + 1, rows], weight[DH:, columns])
    total += nn(spread[2 - 2 * xl, rows], other[:DH])
    total += nn(spread[3 - 2 * xl, rows], other[DH:])
    out_ref[...] = total.astype(bf16)


def call(kernel, shapes, args, specs=None, outs=None, scratch=(), flops=0, bytes_accessed=0, room=12):
    several = isinstance(shapes, (list, tuple))
    args = [
        pltpu.with_memory_space_constraint(arg, pltpu.HBM) if spec is HBM else arg
        for arg, spec in zip(args, specs or [VMEM] * len(args))
    ]
    return pl.pallas_call(
        kernel,
        out_shape=shapes,
        in_specs=specs or [VMEM] * len(args),
        out_specs=outs or ([VMEM] * len(shapes) if several else VMEM),
        scratch_shapes=list(scratch),
        cost_estimate=pl.CostEstimate(
            flops=flops, bytes_accessed=bytes_accessed, transcendentals=0
        ),
        compiler_params=pltpu.CompilerParams(vmem_limit_bytes=room << 20),
    )(*args)


def shape(dims, dtype):
    return jax.ShapeDtypeStruct(dims, dtype)


def hop(x, steps):
    return lax.ppermute(
        x, CHIPS, [(i, i + steps) for i in range(64) if 0 <= i + steps < 64]
    )


def layer(
    tokens,
    view_ids,
    query_weight,
    key_weight,
    value_weight,
    out_weight,
    rate_weight,
    fast_gate,
    fast_up,
    fast_down,
    step_size,
):
    tagged, *weights, theirs = call(
        tag_kernel,
        [shape((GATHERED, FH), bf16)]
        + [shape((768, WIDE), bf16)] * 3
        + [shape((2, 768), bf16), shape((FH, FH), bf16)],
        (
            tokens,
            view_ids.reshape(1, TOK_DEV),
            query_weight,
            key_weight,
            value_weight,
            rate_weight.T,
            out_weight,
        ),
        specs=[HBM] * 7,
        scratch=[pltpu.VMEM((1, TOK_DEV), jnp.int32), pltpu.SemaphoreType.DMA((7,))],
        bytes_accessed=1 << 18,
    )
    whole = lax.all_gather(tagged, ("xl", "core"), axis=0, tiled=True)
    query, packed, rates = call(
        project_kernel,
        [shape((ROWS, DH), bf16), shape((PACKED, FH), bf16), shape((ROWS, 1), f32)],
        (whole, *weights),
        flops=2 * 256 * 768 * 1152,
        bytes_accessed=3 << 20,
    )
    pieces = [packed]
    ahead = behind = packed
    for _ in range(REACH):
        ahead = hop(ahead, 1)
        behind = hop(behind, -1)
        pieces += [ahead, behind]

    sent = call(
        gradient_kernel,
        pltpu.HBM((3 * DH, FH), bf16),
        (packed, rates, fast_gate, fast_up, fast_down),
        outs=HBM,
        scratch=[pltpu.VMEM((3 * DH, FH), bf16), pltpu.SemaphoreType.DMA((3,))],
        flops=2 * 256 * 192 * 384 * 6,
        bytes_accessed=3 << 20,
    ).reshape(8, 72, FH)

    def add(got):
        return call(
            add_kernel,
            pltpu.HBM((8, 72, FH), bf16),
            (got,),
            outs=HBM,
            scratch=[pltpu.VMEM((72, FH), bf16), pltpu.SemaphoreType.DMA((8,))],
            bytes_accessed=1 << 20,
        )

    got = lax.all_to_all(sent, ("xh", "y"), 0, 0, tiled=True)
    sent = add(got)
    got = lax.all_to_all(sent, "z", 0, 0, tiled=True)
    sent = add(got)
    total = lax.all_to_all(sent, ("xh", "y"), 0, 0, tiled=True)
    total = total.reshape(3 * DH, FH)

    fresh = call(
        fresh_kernel,
        shape((3, DH, FH), bf16),
        (total, fast_gate, fast_up, fast_down, step_size),
        specs=[VMEM] + [HBM] * 4,
        scratch=[
            pltpu.VMEM((3, DH, FH), f32),
            pltpu.SMEM((2,), f32),
            pltpu.SemaphoreType.DMA((4,)),
        ],
        flops=10**10,
        bytes_accessed=3 << 20,
    )
    mixed = call(
        blend_kernel,
        shape((ROWS, DH), bf16),
        (query, fresh, *pieces),
        scratch=[pltpu.VMEM((ROWS, len(pieces) * ROWS), f32)],
        flops=4 * 256 * 2304 * 256,
        bytes_accessed=3 << 20,
    )

    other = lax.ppermute(theirs, "xl", [(0, 1), (1, 0)])
    spread = lax.all_gather(mixed, ("xl", "core"), axis=0)
    return call(
        out_kernel,
        shape((TOK_DEV, FH), bf16),
        (spread, out_weight, other),
        flops=2 * 128 * 768 * 384,
        bytes_accessed=2 << 20,
    )


def solution(mesh):
    fine = Mesh(mesh.devices.reshape(2, 4, 8, 2, 2), ("xh", "y", "z", "core", "xl"))
    placed = (
        P(TOK, "xl"),
        P(TOK),
        P(None, "xl"),
        P(None, "xl"),
        P(None, "xl"),
        P("xl", None),
        P(None, "xl"),
        P("xl", None, None),
        P("xl", None, None),
        P("xl", None, None),
        P("xl"),
    )
    return jax.shard_map(layer, mesh=fine, in_specs=placed, out_specs=P(TOK, "xl"), check_vma=False)
```

```python
import jax
import jax.numpy as jnp
from jax import lax
from jax.experimental import pallas as pl
from jax.experimental.pallas import tpu as pltpu
from jax.sharding import Mesh, PartitionSpec as P


NS_STEPS = 5
newton_a = 3.4445
newton_b = -4.775
newton_c = 2.0315
epsilon = 1e-06
masked_score = -1e30

TOK = ("xh", "y", "z", "core")
CHIPS = ("xh", "y", "z")
REACH = 4
DH = 192
FH = 384
TOK_DEV = 128
ROWS = 2 * TOK_DEV
PACKED = ROWS + 16
GATHERED = TOK_DEV + 16
TAGS = 32
WIDE = 256
f32 = jnp.float32
bf16 = jnp.bfloat16
ANY = pl.BlockSpec(memory_space=pl.ANY)
HBM = pl.BlockSpec(memory_space=pltpu.HBM)
VMEM = pl.BlockSpec(memory_space=pltpu.VMEM)
SMEM = pl.BlockSpec(memory_space=pltpu.SMEM)


def normalize(values):
    widened = values.astype(f32)
    scale = lax.rsqrt(jnp.mean(widened * widened, axis=-1, keepdims=True) + epsilon)
    return (widened * scale).astype(bf16)


def halves(x):
    high = x.astype(bf16)
    return high, (x - high.astype(f32)).astype(bf16)


def nt(a, b):
    return lax.dot_general(a, b, (((1,), (1,)), ((), ())), preferred_element_type=f32)


def nn(a, b):
    return lax.dot_general(a, b, (((1,), (0,)), ((), ())), preferred_element_type=f32)


def tn(a, b):
    return lax.dot_general(a, b, (((0,), (0,)), ((), ())), preferred_element_type=f32)


def copies(sem, *pairs):
    started = [
        pltpu.make_async_copy(source, target, sem.at[i]) for i, (source, target) in enumerate(pairs)
    ]
    for copy in started:
        copy.start()
    return started


def tag_kernel(
    tokens, views_hbm, wq_hbm, wk_hbm, wv_hbm, wr_hbm, wo_hbm,
    tagged_ref, wq, wk, wv, wr, theirs, views, sem,
):
    columns = pl.ds(pl.multiple_of((1 - lax.axis_index("xl")) * FH, FH), FH)
    near = pl.ds(pl.multiple_of(lax.axis_index("core") * TOK_DEV, TOK_DEV), WIDE)
    fetches = copies(
        sem,
        (views_hbm, views),
        (tokens, tagged_ref.at[pl.ds(0, TOK_DEV)]),
        (wq_hbm.at[:, near], wq),
        (wk_hbm.at[:, near], wk),
        (wv_hbm.at[:, near], wv),
        (wr_hbm, wr),
        (wo_hbm.at[:, columns], theirs),
    )
    fetches[0].wait()
    row = (views[...] + 1).astype(f32).astype(bf16)
    row = jnp.concatenate((row, jnp.zeros((1, FH - TOK_DEV), bf16)), 1)
    tagged_ref[TOK_DEV:] = jnp.broadcast_to(row, (16, FH))
    for fetch in fetches[1:]:
        fetch.wait()


def project_kernel(whole, wq, wk, wv, wr, query_ref, packed_ref, rates_ref):
    core = lax.axis_index("core")
    chip = (lax.axis_index("xh") * 4 + lax.axis_index("y")) * 8 + lax.axis_index("z")
    left = jnp.concatenate(
        (whole[:TOK_DEV], whole[GATHERED : GATHERED + TOK_DEV]), 0
    )
    base = 2 * GATHERED
    right = jnp.concatenate(
        (whole[base : base + TOK_DEV], whole[base + GATHERED : base + GATHERED + TOK_DEV]), 0
    )
    both_rates = jax.nn.softplus(nt(left, wr[:, :FH]) + nt(right, wr[:, FH:]))
    rates = jnp.where(core == 0, both_rates[:, :1], both_rates[:, 1:])
    rates_ref[...] = rates * jnp.where(chip < 48, 1.0, 0.0)
    tags = jnp.concatenate(
        (whole[TOK_DEV:GATHERED, :TOK_DEV], whole[GATHERED + TOK_DEV : base, :TOK_DEV]), 1
    )
    tags = jnp.concatenate((tags, jnp.zeros((16, FH - ROWS), bf16)), 1)

    def both(w):
        return nn(left, w[:FH]) + nn(right, w[FH:])

    def own(w):
        product = both(w)
        return jnp.where(core == 0, product[:, :DH], product[:, WIDE - DH :]).astype(bf16)

    packed_ref[:ROWS] = jnp.concatenate((own(wk), own(wv)), 1)
    packed_ref[ROWS:] = tags
    query_ref[...] = own(wq)


def gradient_kernel(packed, rates, gate_ref, up_ref, down_ref, sent_hbm, sent_ref, sem):
    core = lax.axis_index("core")
    keys_n = normalize(packed[:ROWS, :DH])
    value = packed[:ROWS, DH:].astype(f32)
    gate = nn(keys_n, gate_ref[core].astype(bf16))
    upward = nn(keys_n, up_ref[core].astype(bf16))
    logistic = jax.nn.sigmoid(gate)
    active = gate * logistic
    product = (active * upward).astype(bf16)
    error = (-rates[...] * value).astype(bf16)
    stores = []

    def send(i, part):
        rows = pl.ds(i * DH, DH)
        sent_ref[rows] = part.astype(bf16)
        stores.append(pltpu.make_async_copy(sent_ref.at[rows], sent_hbm.at[rows], sem.at[i]))
        stores[-1].start()

    send(2, tn(error, product))
    back = nn(error, down_ref[core].astype(bf16))
    send(1, tn(keys_n, (back * active).astype(bf16)))
    grad_g = (back * upward * logistic * (1.0 + gate * (1.0 - logistic))).astype(bf16)
    send(0, tn(keys_n, grad_g))
    for store in stores:
        store.wait()


def add_kernel(got, sent_ref):
    part = got[0].astype(f32)
    for i in range(1, 8):
        part = part + got[i].astype(f32)
    part = part.astype(bf16)
    for i in range(8):
        sent_ref[i] = part


def blend_kernel(query_ref, fresh, *refs):
    pieces, mixed_ref, scores_ref = refs[: 2 * REACH + 1], refs[-2], refs[-1]
    query = query_ref[...]
    numbers = lax.broadcasted_iota(jnp.int32, (TAGS, ROWS), 0).astype(f32)

    def marks(piece):
        return jnp.where(numbers == piece[ROWS : ROWS + 1, :ROWS].astype(f32), 1.0, 0.0).astype(bf16)

    own_marks = marks(pieces[0])
    own_marks = jnp.where(numbers > 0.5, own_marks, jnp.zeros_like(own_marks))
    peak = None
    for p, piece in enumerate(pieces):
        scores = nt(query, piece[:ROWS, :DH]) * DH**-0.5
        scores = jnp.where(tn(own_marks, marks(piece)) > 0.5, scores, masked_score)
        scores_ref[:, p * ROWS : (p + 1) * ROWS] = scores
        high = jnp.max(scores, axis=-1, keepdims=True)
        peak = high if peak is None else jnp.maximum(peak, high)
    mass = None
    for p in range(len(pieces)):
        weights = jnp.exp(scores_ref[:, p * ROWS : (p + 1) * ROWS] - peak)
        scores_ref[:, p * ROWS : (p + 1) * ROWS] = weights
        one = jnp.sum(weights, axis=-1, keepdims=True)
        mass = one if mass is None else mass + one
    inverse = 1.0 / mass
    total = None
    for p, piece in enumerate(pieces):
        weights = (scores_ref[:, p * ROWS : (p + 1) * ROWS] * inverse).astype(bf16)
        one = nn(weights, piece[:ROWS, DH:])
        total = one if total is None else total + one
    queries_n = normalize(query)
    gate = nn(queries_n, fresh[0])
    upward = nn(queries_n, fresh[1])
    product = (gate * jax.nn.sigmoid(gate) * upward).astype(bf16)
    mixed_ref[...] = (total + nt(product, fresh[2])).astype(bf16)


def fresh_kernel(total_ref, gate_hbm, up_hbm, down_hbm, step_hbm, fresh_ref, masters, step_ref, sem):
    core = lax.axis_index("core")
    fetches = copies(
        sem,
        (gate_hbm.at[core], masters.at[0]),
        (up_hbm.at[core], masters.at[1]),
        (down_hbm.at[core], masters.at[2]),
        (step_hbm, step_ref),
    )
    currents = []
    for m in range(3):
        matrix = total_ref[m * DH : (m + 1) * DH].astype(f32)
        length = jnp.sqrt(jnp.sum(matrix * matrix))
        currents.append(matrix / (length + epsilon))
    for _ in range(NS_STEPS):
        squares = []
        for x in currents:
            h, l = halves(x)
            cross = nt(h, l)
            squares.append((h, l, nt(h, h) + (cross + cross.T)))
        mixers = []
        for h, l, a in squares:
            ah, al = halves(a)
            aa = nn(ah, ah) + (nn(ah, al) + nn(al, ah))
            mixers.append((h, l, newton_b * a + newton_c * aa))
        nexts = []
        for x, (h, l, b) in zip(currents, mixers):
            bh, bl = halves(b)
            wide = nn(bh, jnp.concatenate((h, l), 1))
            nexts.append(newton_a * x + (wide[:, :FH] + (wide[:, FH:] + nn(bl, h))))
        currents = nexts
    for fetch in fetches:
        fetch.wait()
    step = step_ref[core]
    for m in range(3):
        fresh_ref[m] = (masters[m] - step * currents[m]).astype(bf16)


def out_kernel(spread, weight, other, out_ref):
    core = lax.axis_index("core")
    xl = lax.axis_index("xl")
    rows = pl.ds(pl.multiple_of(core * TOK_DEV, TOK_DEV), TOK_DEV)
    columns = pl.ds(pl.multiple_of(xl * FH, FH), FH)
    total = nn(spread[2 * xl, rows], weight[:DH, columns])
    total += nn(spread[2 * xl + 1, rows], weight[DH:, columns])
    total += nn(spread[2 - 2 * xl, rows], other[:DH])
    total += nn(spread[3 - 2 * xl, rows], other[DH:])
    out_ref[...] = total.astype(bf16)


def call(kernel, shapes, args, specs=None, outs=None, scratch=(), flops=0, bytes_accessed=0, room=12):
    several = isinstance(shapes, (list, tuple))
    args = [
        pltpu.with_memory_space_constraint(arg, pltpu.HBM) if spec is HBM else arg
        for arg, spec in zip(args, specs or [VMEM] * len(args))
    ]
    return pl.pallas_call(
        kernel,
        out_shape=shapes,
        in_specs=specs or [VMEM] * len(args),
        out_specs=outs or ([VMEM] * len(shapes) if several else VMEM),
        scratch_shapes=list(scratch),
        cost_estimate=pl.CostEstimate(
            flops=flops, bytes_accessed=bytes_accessed, transcendentals=0
        ),
        compiler_params=pltpu.CompilerParams(vmem_limit_bytes=room << 20),
    )(*args)


def shape(dims, dtype):
    return jax.ShapeDtypeStruct(dims, dtype)


def hop(x, steps):
    return lax.ppermute(
        x, CHIPS, [(i, i + steps) for i in range(64) if 0 <= i + steps < 64]
    )


def layer(
    tokens,
    view_ids,
    query_weight,
    key_weight,
    value_weight,
    out_weight,
    rate_weight,
    fast_gate,
    fast_up,
    fast_down,
    step_size,
):
    tagged, *weights, theirs = call(
        tag_kernel,
        [shape((GATHERED, FH), bf16)]
        + [shape((768, WIDE), bf16)] * 3
        + [shape((2, 768), bf16), shape((FH, FH), bf16)],
        (
            tokens,
            view_ids.reshape(1, TOK_DEV),
            query_weight,
            key_weight,
            value_weight,
            rate_weight.T,
            out_weight,
        ),
        specs=[HBM] * 7,
        scratch=[pltpu.VMEM((1, TOK_DEV), jnp.int32), pltpu.SemaphoreType.DMA((7,))],
        bytes_accessed=1 << 18,
    )
    whole = lax.all_gather(tagged, ("xl", "core"), axis=0, tiled=True)
    query, packed, rates = call(
        project_kernel,
        [shape((ROWS, DH), bf16), shape((PACKED, FH), bf16), shape((ROWS, 1), f32)],
        (whole, *weights),
        flops=2 * 256 * 768 * 1152,
        bytes_accessed=3 << 20,
    )
    pieces = [packed]
    ahead = behind = packed
    for _ in range(REACH):
        ahead = hop(ahead, 1)
        behind = hop(behind, -1)
        pieces += [ahead, behind]

    sent = call(
        gradient_kernel,
        pltpu.HBM((3 * DH, FH), bf16),
        (packed, rates, fast_gate, fast_up, fast_down),
        outs=HBM,
        scratch=[pltpu.VMEM((3 * DH, FH), bf16), pltpu.SemaphoreType.DMA((3,))],
        flops=2 * 256 * 192 * 384 * 6,
        bytes_accessed=3 << 20,
    ).reshape(8, 72, FH)

    def add(got):
        return call(add_kernel, shape((8, 72, FH), bf16), (got,), bytes_accessed=1 << 20)

    got = lax.all_to_all(sent, ("xh", "y"), 0, 0, tiled=True)
    sent = add(got)
    got = lax.all_to_all(sent, "z", 0, 0, tiled=True)
    sent = add(got)
    total = lax.all_to_all(sent, ("xh", "y"), 0, 0, tiled=True)
    total = total.reshape(3 * DH, FH)

    fresh = call(
        fresh_kernel,
        shape((3, DH, FH), bf16),
        (total, fast_gate, fast_up, fast_down, step_size),
        specs=[VMEM] + [HBM] * 4,
        scratch=[
            pltpu.VMEM((3, DH, FH), f32),
            pltpu.SMEM((2,), f32),
            pltpu.SemaphoreType.DMA((4,)),
        ],
        flops=10**10,
        bytes_accessed=3 << 20,
    )
    mixed = call(
        blend_kernel,
        shape((ROWS, DH), bf16),
        (query, fresh, *pieces),
        scratch=[pltpu.VMEM((ROWS, len(pieces) * ROWS), f32)],
        flops=4 * 256 * 2304 * 256,
        bytes_accessed=3 << 20,
    )

    other = lax.ppermute(theirs, "xl", [(0, 1), (1, 0)])
    spread = lax.all_gather(mixed, ("xl", "core"), axis=0)
    return call(
        out_kernel,
        shape((TOK_DEV, FH), bf16),
        (spread, out_weight, other),
        flops=2 * 128 * 768 * 384,
        bytes_accessed=2 << 20,
    )


def solution(mesh):
    fine = Mesh(mesh.devices.reshape(2, 4, 8, 2, 2), ("xh", "y", "z", "core", "xl"))
    placed = (
        P(TOK, "xl"),
        P(TOK),
        P(None, "xl"),
        P(None, "xl"),
        P(None, "xl"),
        P("xl", None),
        P(None, "xl"),
        P("xl", None, None),
        P("xl", None, None),
        P("xl", None, None),
        P("xl"),
    )
    return jax.shard_map(layer, mesh=fine, in_specs=placed, out_specs=P(TOK, "xl"), check_vma=False)
```
